256 devices in a mesh: dp: 128 (over y, z, x), grp: 2 (over core).
Axes of the slice: x: 4, y: 4, z: 8, core: 2. Of those that a mesh axis runs over, the one named last changes fastest.
Arguments:
- embeddings: bfloat16 [65536, 1024], P(('dp', 'grp')), may hold values from -6 to 6
- owner_dest: int32 [65536, 1], P(('dp', 'grp')), may hold values from 0 to 127; in each aligned block of 256 rows (0 to 255, 256 to 511, ...) at most 6 rows name the same one
- cluster_slot: int32 [65536, 1], P(('dp', 'grp')), may hold values from 0 to 7
- cluster_rank: int32 [1024], replicated, may hold values from 0 to 1023, each once
- centroids: bfloat16 [1024, 1024], P('dp'), may hold values from -2 to 2
Outputs:
- shift: bfloat16 [1024, 1792], replicated
- moment: float32 [1024, 256, 256], P(('dp', 'grp'))
The draws below stay inside these ranges and needn't reach their ends.
Inputs may be any that keep to these rules, and one draw needn't show every extreme that they name: `owner_dest`: among the rows of one device (aligned blocks of 256 rows), no owner is named by more than 6 rows, a bound that some block reaches. `cluster_rank`: A permutation.
All inputs are finite; a program needn't handle non-finite values.
Results may differ from the reference program's by a relative error of at most 0.0034.
Values may be sent and summed in bfloat16 or wider, within the bound.
A program may use at most 64 MiB of HBM per device.

```python
import math
import jax
import jax.numpy as jnp
import numpy as np
from jax import lax

D = 1024
D_SMALL = 256
D_MID = 512
WIDE = 1792
ROWS_DEV = 256
CL_DEV = 8
K = 1024
CAP = 6
TOTAL = 65536
N_DP = 128


def plant(drawn, key, low, largest):
    place = [jax.random.randint(jax.random.fold_in(key, axis), (), 0, length) for axis, length in enumerate(drawn.shape)]
    longest = drawn.shape.index(max(drawn.shape))
    beside = place[:longest] + [(place[longest] + 1) % drawn.shape[longest]] + place[longest + 1:]
    return drawn.at[tuple(place)].set(low).at[tuple(beside)].set(largest)


def block_levels(stream_key, extent, cuts, low, largest):
    factor_of = 1.0
    for axis_at, parts in cuts:
        draws = jax.random.uniform(jax.random.fold_in(jax.random.fold_in(stream_key, 6), axis_at), (parts,), jnp.float32, low / len(cuts), largest / len(cuts))
        factor_of = factor_of * jnp.repeat(jnp.exp(draws), extent[axis_at] // parts).reshape((-1,) + (1,) * (len(extent) - 1 - axis_at))
    return factor_of


def routed_block(stream_key, own, number, rows, number_of, top, limit, lean):
    order = jax.random.permutation(stream_key, number_of)
    packed, common = load_shares(number_of, rows * top, limit, lean, True), load_shares(number_of, rows * top, limit, lean, False)
    places = jnp.arange(number_of)

    def named(sizes, turn):
        used = int((sizes > 0).sum())
        fixed = max(1, used // 4)
        shifted = fixed + (places - fixed + turn * (used - fixed)) % max(1, number_of - fixed)
        return jnp.zeros((number_of,), jnp.int32).at[order[jnp.where(places < fixed, places, shifted)]].set(jnp.asarray(sizes, jnp.int32))

    sizes = jnp.where(number % 4 == 0, named(packed, number // 4), named(common, number - number // 4 - 1))
    mixed = jax.random.permutation(jax.random.fold_in(own, 3), number_of)
    source_of, receiver = mixed[0:number_of // 2 * 2:2], mixed[1:number_of // 2 * 2:2]
    room = jnp.minimum(sizes[source_of] - 1, limit - sizes[receiver]) // 2
    room = jnp.where((source_of == order[0]) | (receiver == order[0]) | (sizes[receiver] == 0), 0, jnp.maximum(room, 0))
    shifted = jax.random.randint(jax.random.fold_in(own, 4), (number_of // 2,), 0, 1 << 20) % (room + 1)
    sizes = sizes.at[source_of].add(-shifted).at[receiver].add(shifted)
    items = jnp.searchsorted(jnp.cumsum(sizes), jnp.arange(rows * top), side="right").astype(jnp.int32)
    grid = items.reshape(top, rows).T
    grid = grid[jax.random.permutation(jax.random.fold_in(own, 1), rows)]
    turn = jax.random.randint(jax.random.fold_in(own, 2), (rows, 1), 0, top)
    return jnp.take_along_axis(grid, (jnp.arange(top)[None, :] + turn) % top, axis=1)


def load_shares(number_of, total, bound, skew, full):
    portions = [(1 << 20) // math.isqrt(rank ** skew) + 1 for rank in range(1, number_of + 1)]
    largest = bound if full else min(bound, max(-(-total // number_of), total * portions[0] // sum(portions)))
    least = 1 if total - largest >= number_of - 1 else 0
    given, spare = [largest] + [least] * (number_of - 1), total - largest - least * (number_of - 1)
    while spare > 0:
        candidates = [i for i in range(1, number_of) if given[i] < largest] or [i for i in range(1, number_of) if given[i] < bound]
        whole, left = sum([portions[i] for i in candidates]), spare
        for i in candidates:
            extra = min(bound - given[i], max(1, left * portions[i] // whole), spare)
            given[i] = given[i] + extra
            spare = spare - extra
    return np.array(given)


def bell_draw(stream_key, dims, spread, limit, cuts=(), held_as=jnp.bfloat16):
    array = spread * jax.random.normal(stream_key, dims, jnp.float32)
    if cuts:
        array = array * block_levels(stream_key, dims, cuts, -0.22, 0.18)
    return jnp.clip(array, -limit, limit).astype(held_as)


def setup_inputs(seed: int = 0) -> dict:
    splits = jax.random.split(jax.random.key(seed), 6)
    embeddings = bell_draw(splits[0], (TOTAL, D), 1.0, 6.0, ((0, 256),))
    owner_dest_keys = jax.random.split(jax.random.fold_in(splits[1], 1), TOTAL // ROWS_DEV)
    owner_dest_turns = jax.random.permutation(jax.random.fold_in(splits[1], 3), TOTAL // ROWS_DEV)
    owner_dest = jax.vmap(lambda own, number: routed_block(jax.random.fold_in(splits[1], 2), own, number, ROWS_DEV, N_DP, 1, CAP, 2))(owner_dest_keys, owner_dest_turns).reshape((TOTAL, 1))
    cluster_slot = plant(jax.random.randint(splits[2], (TOTAL, 1), 0, CL_DEV), jax.random.fold_in(splits[2], 1), 0, CL_DEV - 1).astype(jnp.int32)
    cluster_rank = jax.random.permutation(splits[3], K).astype(jnp.int32)
    centroids = bell_draw(splits[4], (K, D), 0.3, 2.0, ((0, 128),))
    return {"embeddings": embeddings, "owner_dest": owner_dest, "cluster_slot": cluster_slot, "cluster_rank": cluster_rank, "centroids": centroids}


def residuals(rows, cent):
    pieces = []
    for width in (D_SMALL, D_MID, D):
        part = rows[:, :width]
        scale = lax.rsqrt(lax.optimization_barrier(jnp.mean(part * part, axis=-1, keepdims=True)) + 1e-06)
        pieces.append(part * scale - cent[:, :width])
    return jnp.concatenate(pieces, axis=1).astype(jnp.bfloat16)

def reference(embeddings, owner_dest, cluster_slot, cluster_rank, centroids):
    rank = (owner_dest[:, 0] * CL_DEV + cluster_slot[:, 0]).astype(jnp.int32)
    block = 256
    count_blocks = TOTAL // block

    def advance(carry, index):
        sums, counts, grams = carry
        start = (index * block).astype(jnp.int32)
        rows = lax.dynamic_slice_in_dim(embeddings, start, block, 0).astype(jnp.float32)
        ranks = lax.dynamic_slice_in_dim(rank, start, block, 0)
        cent = centroids[ranks].astype(jnp.float32)
        resid = residuals(rows, cent).astype(jnp.float32)
        sums = sums + jax.ops.segment_sum(resid, ranks, num_segments=K)
        counts = counts + jax.ops.segment_sum(jnp.ones((block,), jnp.float32), ranks, num_segments=K)
        small = resid[:, :D_SMALL]
        outer = small[:, :, None] * small[:, None, :]
        grams = grams + jax.ops.segment_sum(outer, ranks, num_segments=K)
        return ((sums, counts, grams), None)
    start_carry = (jnp.zeros((K, WIDE), jnp.float32), jnp.zeros((K,), jnp.float32), jnp.zeros((K, D_SMALL, D_SMALL), jnp.float32))
    (sums, counts, grams), _ = lax.scan(advance, start_carry, jnp.arange(count_blocks, dtype=jnp.int32))
    denom = counts + 1.0
    table = (sums / denom[:, None]).astype(jnp.bfloat16)
    shift = table[cluster_rank]
    moment = grams / denom[:, None, None]
    return (shift, moment)
```

```python
import functools

import jax
import jax.numpy as jnp
from jax import lax
from jax.experimental import pallas as pl
from jax.experimental.pallas import tpu as pltpu
from jax.sharding import PartitionSpec as P

D = 1024
D_SMALL = 256
D_MID = 512
WIDE = 1792
HALF = 896
NX, NY, NZ = 4, 4, 8
MESH = pl.DeviceIdType.MESH


def residuals(rows, cent):
    rows = rows.astype(jnp.float32)
    pieces = []
    for width in (D_SMALL, D_MID, D):
        part = rows[:, :width]
        scale = lax.rsqrt(jnp.mean(part * part, axis=-1, keepdims=True) + 1e-06)
        pieces.append(part * scale - cent[:, :width])
    return jnp.concatenate(pieces, axis=1).astype(jnp.bfloat16)


def slot_onehot(slots, per_owner):
    return (slots[:, None] == jnp.arange(per_owner, dtype=jnp.int32)[None, :]).astype(jnp.bfloat16)


def moments(select, small):
    count_rows = small.shape[0]
    per_owner = select.shape[1]
    spread = (select[:, :, None] * small[:, None, :]).reshape(count_rows, per_owner * D_SMALL)
    gram = jnp.einsum("sa,sb->ab", spread, small, preferred_element_type=jnp.float32)
    return gram.reshape(per_owner, D_SMALL, D_SMALL)


def gather_table(blk_ref, out_ref, own_sem, zs, zr, as_, ar, ps, pr):
    dp = lax.axis_index("dp")
    g = lax.axis_index("grp")
    x = dp % NX
    z = (dp // NX) % NZ
    y = dp // (NX * NZ)
    h = 1 - g

    def dev(yy, zz, xx, gg):
        return ((yy * NZ + zz) * NX + xx, gg)

    def place(i, j):
        return (y + 4 + i * g + j * h) % NY, (x + 4 + i * h + j * g) % NX

    cols = pl.ds(pl.multiple_of(g * HALF, 128), HALF)
    pcols = pl.ds(pl.multiple_of(h * HALF, 128), HALF)

    def chunk(i, j, z0=0, nz=NZ, at=cols):
        yy, xx = place(i, j)
        return out_ref.at[yy, pl.ds(z0, nz), xx, :, at]

    def to(i, j):
        yy, xx = place(i, j)
        return dev(yy, z, xx, g)

    partner = dev(y, z, x, h)
    zpeers = [dev(y, (z + d) % NZ, x, g) for d in range(1, NZ)]
    barrier = pltpu.get_barrier_semaphore()
    peers = zpeers + [to(1, 0), to(-1, 0), to(0, 1), to(0, -1), partner]
    for peer in peers:
        pl.semaphore_signal(barrier, inc=1, device_id=peer, device_id_type=MESH)
    pl.semaphore_wait(barrier, len(peers))

    sent = []

    def send(src, dst, ss, rs, peer):
        c = pltpu.make_async_remote_copy(src_ref=src, dst_ref=dst, send_sem=ss, recv_sem=rs,
                                         device_id=peer, device_id_type=MESH)
        c.start()
        sent.append(c)
        return c

    mine = out_ref.at[y, z, x, :, cols]
    zc = []
    for d in range(1, NZ):
        zc.append(send(blk_ref, mine, zs.at[d - 1], zr.at[d - 1], zpeers[d - 1]))
    own = pltpu.make_async_copy(blk_ref, mine, own_sem)
    own.start()
    own.wait()

    def got(ref, sem):
        pltpu.make_async_copy(ref, ref, sem).wait()

    for d in range(1, NZ):
        got(mine, zr.at[d - 1])

    order = [0, -1, 1, 2]
    pn = [0]
    partner_chunks = []

    def share(i, j):
        k = pn[0]
        pn[0] += 1
        send(chunk(i, j), chunk(i, j), ps.at[k], pr.at[k], partner)

    def ring_out(row, here, plus, minus):
        send(here, here, as_.at[row, 0], ar.at[row, 0], plus)
        send(here, here, as_.at[row, 1], ar.at[row, 1], minus)

    def first(i):
        return to(1, 0) if i > 0 else to(-1, 0)

    ring_out(0, chunk(0, 0), to(1, 0), to(-1, 0))
    ring_out(1, chunk(0, 0), to(0, 1), to(0, -1))
    share(0, 0)
    got(chunk(-1, 0), ar.at[0, 0])
    low = chunk(-1, 0, 0, 4)
    send(low, low, as_.at[0, 2], ar.at[0, 2], to(1, 0))
    ring_out(2, chunk(-1, 0), to(0, 1), to(0, -1))
    share(-1, 0)
    got(chunk(1, 0), ar.at[0, 1])
    high = chunk(1, 0, 4, 4)
    send(high, high, as_.at[0, 3], ar.at[0, 3], to(-1, 0))
    ring_out(3, chunk(1, 0), to(0, 1), to(0, -1))
    share(1, 0)

    def second(row, i):
        got(chunk(i, -1), ar.at[row, 0])
        lo = chunk(i, -1, 0, 4)
        send(lo, lo, as_.at[row, 2], ar.at[row, 2], to(0, 1))
        share(i, -1)
        got(chunk(i, 1), ar.at[row, 1])
        hi = chunk(i, 1, 4, 4)
        send(hi, hi, as_.at[row, 3], ar.at[row, 3], to(0, -1))
        share(i, 1)

    second(1, 0)
    got(chunk(2, 0, 0, 4), ar.at[0, 2])
    got(chunk(2, 0, 4, 4), ar.at[0, 3])
    ring_out(4, chunk(2, 0), to(0, 1), to(0, -1))
    share(2, 0)
    second(2, -1)
    second(3, 1)
    second(4, 2)
    for row, i in ((1, 0), (2, -1), (3, 1), (4, 2)):
        got(chunk(i, 2, 0, 4), ar.at[row, 2])
        got(chunk(i, 2, 4, 4), ar.at[row, 3])
        share(i, 2)
    for k in range(16):
        got(chunk(0, 0, at=pcols), pr.at[k])
    for c in sent:
        c.wait_send()


def all_tables(block):
    dma = pltpu.SemaphoreType.DMA
    out = pl.pallas_call(
        gather_table,
        out_shape=jax.ShapeDtypeStruct((NY, NZ, NX, 8, WIDE), jnp.bfloat16),
        in_specs=[pl.BlockSpec(memory_space=pltpu.VMEM)],
        out_specs=pl.BlockSpec(memory_space=pltpu.VMEM),
        scratch_shapes=[dma, dma((7,)), dma((7,)), dma((5, 4)), dma((5, 4)), dma((16,)), dma((16,))],
        compiler_params=pltpu.CompilerParams(collective_id=1, has_side_effects=True),
        name="gather_table",
    )(block)
    return out.reshape(NY * NZ * NX * 8, WIDE)


def on_device(embeddings, owner_dest, cluster_slot, cluster_rank, centroids):
    rows_here = embeddings.shape[0]
    width = embeddings.shape[1]
    owners = lax.axis_size("dp")
    per_owner = centroids.shape[0]
    capacity = 3 * rows_here // owners
    dest = owner_dest[:, 0]
    slot = cluster_slot[:, 0]
    hits = (dest[:, None] == jnp.arange(owners, dtype=jnp.int32)[None, :]).astype(jnp.int32)
    before = jnp.cumsum(hits, axis=0) - hits
    position = jnp.sum(before * hits, axis=1)
    target = dest * capacity + position

    def pack(values, fill):
        buffer = jnp.full((owners * capacity,) + values.shape[1:], fill, values.dtype)
        buffer = buffer.at[target].set(values)
        return buffer.reshape((owners, capacity) + values.shape[1:])

    sent_ids = pack(slot, -1)
    sent_rows = pack(embeddings, 0)
    got_rows = lax.all_to_all(sent_rows, "dp", split_axis=0, concat_axis=0, tiled=True)
    got_ids = lax.all_to_all(sent_ids, "dp", split_axis=0, concat_axis=0, tiled=True)
    flat_ids = got_ids.reshape(-1)
    select = slot_onehot(flat_ids, per_owner)
    cent = jnp.dot(select, centroids, preferred_element_type=jnp.float32)
    resid = residuals(got_rows.reshape(-1, width), cent)
    sums = jnp.einsum("sc,sw->cw", select, resid, preferred_element_type=jnp.float32)
    counts = jnp.sum(select.astype(jnp.float32), axis=0)
    gram = moments(select, resid[:, :D_SMALL])
    counts = lax.psum(counts, "grp")
    sums_part = lax.psum_scatter(sums, "grp", scatter_dimension=1, tiled=True)
    gram_part = lax.psum_scatter(gram, "grp", scatter_dimension=0, tiled=True)
    denom = counts + 1.0
    table_part = (sums_part / denom[:, None]).astype(jnp.bfloat16)
    table = all_tables(table_part)
    pick = (cluster_rank[:, None] == jnp.arange(table.shape[0], dtype=jnp.int32)[None, :]).astype(jnp.bfloat16)
    shift = jnp.dot(pick, table, preferred_element_type=jnp.float32).astype(jnp.bfloat16)
    g = lax.axis_index("grp")
    mine = lax.dynamic_slice_in_dim(denom, g * (per_owner // 2), per_owner // 2, 0)
    moment = gram_part / mine[:, None, None]
    return (shift, moment)


def solution(mesh):
    placed = (
        P(("dp", "grp"), None),
        P(("dp", "grp"), None),
        P(("dp", "grp"), None),
        P(),
        P("dp", None),
    )
    return jax.shard_map(
        on_device,
        mesh=mesh,
        in_specs=placed,
        out_specs=(P(), P(("dp", "grp"), None, None)),
        check_vma=False,
    )
```

```python
import functools

import jax
import jax.numpy as jnp
from jax import lax
from jax.experimental import pallas as pl
from jax.experimental.pallas import tpu as pltpu
from jax.sharding import PartitionSpec as P

WIDE = 1792
HALF = 896
NX, NY, NZ = 4, 4, 8
CHIPS = 128
SM = 256
MESH = pl.DeviceIdType.MESH
F32 = jnp.float32
BF16 = jnp.bfloat16
EPS = 1e-06


def iota(shape, dim):
    return lax.broadcasted_iota(jnp.int32, shape, dim)


def thirds(v):
    hi = v.astype(BF16)
    rest = v - hi.astype(F32)
    mid = rest.astype(BF16)
    return hi, mid, (rest - mid.astype(F32)).astype(BF16)


def row_of(col):
    n = col.shape[0]
    eye = iota((n, n), 0) == iota((n, n), 1)
    return jnp.sum(jnp.where(eye, col, 0.0), axis=0, keepdims=True)


def scales(rows):
    sq = rows * rows
    s512 = jnp.sum(sq[:, :512], axis=1, keepdims=True)
    s1024 = s512 + jnp.sum(sq[:, 512:], axis=1, keepdims=True)
    return lax.rsqrt(s512 * (1.0 / 512) + EPS), lax.rsqrt(s1024 * (1.0 / 1024) + EPS)


def pack(emb_ref, dest_ref, slot_ref, sendbuf):
    n = emb_ref.shape[0]
    dest = dest_ref[...]
    slot = slot_ref[...]
    destf = dest.astype(F32)
    hits = dest == iota((n, CHIPS), 1)
    lower = (iota((n, n), 1) < iota((n, n), 0)).astype(BF16)
    before = jnp.dot(lower, hits.astype(F32).astype(BF16), preferred_element_type=F32)
    pos = jnp.sum(jnp.where(hits, before, 0.0), axis=1, keepdims=True)
    target = row_of(destf * 8.0 + pos).astype(jnp.int32)
    destrow = row_of(destf).astype(jnp.int32)
    s512, s1024 = scales(emb_ref[...].astype(F32))
    values = [slot.astype(F32) + 1.0]
    for s in (s512, s1024):
        values += [t.astype(F32) for t in thirds(s)]
    lane = iota((n, 128), 1)
    tags = jnp.zeros((n, 128), F32)
    for q, v in enumerate(values):
        tags = jnp.where((lane & 15) == q, v, tags)
    tags = jnp.where((lane >> 4) == pos.astype(jnp.int32), tags, 0.0).astype(BF16)
    owner = (iota((CHIPS, n), 0) == destrow).astype(F32).astype(BF16)
    tags = jnp.dot(owner, tags, preferred_element_type=F32)
    place = (iota((CHIPS * 8, n), 0) == target).astype(F32).astype(BF16)
    rows = jnp.dot(place, emb_ref[:, :SM], preferred_element_type=F32).reshape(CHIPS, 8, SM)
    wide = jnp.concatenate([tags, jnp.zeros((CHIPS, SM - 128), F32)], axis=1)
    rows = jnp.where(iota((CHIPS, 8, SM), 1) == 6, wide[:, None, :], rows)
    sendbuf[...] = rows.astype(BF16)


def whole(embs, dests, slots, g, total):
    hots, las, lbs = [], [], []
    for emb_ref, dest_ref, slot_ref in zip(embs, dests, slots):
        dest = dest_ref[...]
        xx, zz, yy = dest & 3, (dest >> 2) & 7, dest >> 5
        a = xx * (1 - g) + yy * g
        b = yy * (1 - g) + xx * g
        order = ((a * 4 + b) * 8 + zz) * 8 + slot_ref[...]
        hots.append(row_of(order.astype(F32)))
        s512, s1024 = scales(emb_ref[...].astype(F32))
        gf = g.astype(F32)
        sa = s512 * (1.0 - gf) + s1024 * gf
        ca = pl.ds(pl.multiple_of(256 + g * 256, 256), 256)
        cb = pl.ds(pl.multiple_of(256 + g * 512, 256), 256)
        las.append(thirds(emb_ref[:, ca].astype(F32) * sa))
        lbs.append(thirds(emb_ref[:, cb].astype(F32) * s1024))
    order = jnp.concatenate(hots, axis=1).astype(jnp.int32)
    k = 8 * CHIPS
    hot = (iota((k, order.shape[1]), 0) == order).astype(F32).astype(BF16)
    for at, parts in ((0, las), (256, lbs)):
        acc = jnp.zeros((k, 256), F32)
        for t in range(3):
            x = jnp.concatenate([p[t] for p in parts], axis=0)
            acc = acc + jnp.dot(hot, x, preferred_element_type=F32)
        total[:, :, :, :, at:at + 256] = acc.reshape(4, 4, NZ, 8, 256)


def routed(emb_ref, dest_ref, slot_ref, cent_ref, table_ref, gram_ref,
           sendbuf, recvbuf, pemb, pdest, pslot, total, half1, full1, half2, full2, zgot, blk, psums, osums,
           pgram, ogram,
           own_sem, a2s, a2r, xs, xr, r1s, r1r, r2s, r2r, z3s, z3r, pss, psr, pgs, pgr,
           zs, zr, as_, ar, ps, pr):
    dp = lax.axis_index("dp")
    g = lax.axis_index("grp")
    x = dp % NX
    z = (dp // NX) % NZ
    y = dp // (NX * NZ)
    h = 1 - g
    partner = (dp, h)
    barrier = pltpu.get_barrier_semaphore()
    pl.semaphore_signal(barrier, inc=1, device_id=partner, device_id_type=MESH)

    def chip(d):
        return (((y + d // 32) % NY) * NZ + (z + (d // 4) % NZ) % NZ) * NX + (x + d % 4) % NX

    def greet(d, c):
        pl.semaphore_signal(barrier, inc=1, device_id=(chip(d), g), device_id_type=MESH)
        return c

    lax.fori_loop(1, CHIPS, greet, 0)
    pack(emb_ref, dest_ref, slot_ref, sendbuf)
    pl.semaphore_wait(barrier, CHIPS)

    sent = []

    def send(src, dst, ss, rs, peer):
        c = pltpu.make_async_remote_copy(src_ref=src, dst_ref=dst, send_sem=ss, recv_sem=rs,
                                         device_id=peer, device_id_type=MESH)
        c.start()
        sent.append(c)

    def got(ref, sem):
        pltpu.make_async_copy(ref, ref, sem).wait()

    send(emb_ref, pemb, xs.at[0], xr.at[0], partner)
    send(dest_ref, pdest, xs.at[1], xr.at[1], partner)
    send(slot_ref, pslot, xs.at[2], xr.at[2], partner)
    mine = pltpu.make_async_copy(sendbuf.at[dp], recvbuf.at[dp], own_sem.at[0])
    mine.start()

    def scatter(d, c):
        t = chip(d)
        pltpu.make_async_remote_copy(src_ref=sendbuf.at[t], dst_ref=recvbuf.at[dp], send_sem=a2s, recv_sem=a2r,
                                     device_id=(t, g), device_id_type=MESH).start()
        return c

    lax.fori_loop(1, CHIPS, scatter, 0)
    got(pemb, xr.at[0])
    got(pdest, xr.at[1])
    got(pslot, xr.at[2])
    whole((emb_ref, pemb), (dest_ref, pdest), (slot_ref, pslot), g, total)

    def to(i, j):
        yy, xx = (y + 4 + i * g + j * h) % NY, (x + 4 + i * h + j * g) % NX
        return ((yy * NZ + z) * NX + xx, g)

    p = x * h + y * g
    q = y * h + x * g

    def ring(at, me, lo, hi, half, full, plus, minus, ss, rs):
        up, down, far = (me + 1) % 4, (me + 3) % 4, (me + 2) % 4
        send(at(far, lo), half.at[0], ss.at[0], rs.at[0], plus)
        send(at(far, hi), half.at[1], ss.at[1], rs.at[1], minus)
        send(at(up, hi), full.at[0, hi], ss.at[2], rs.at[2], plus)
        send(at(down, lo), full.at[1, lo], ss.at[3], rs.at[3], minus)
        got(half.at[0], rs.at[0])
        ref = at(up, lo)
        ref[...] = ref[...] + half[0]
        send(ref, full.at[0, lo], ss.at[4], rs.at[4], plus)
        got(half.at[1], rs.at[1])
        ref = at(down, hi)
        ref[...] = ref[...] + half[1]
        send(ref, full.at[1, hi], ss.at[5], rs.at[5], minus)
        got(full.at[0, hi], rs.at[2])
        got(full.at[1, lo], rs.at[3])
        got(full.at[0, lo], rs.at[4])
        got(full.at[1, hi], rs.at[5])
        for part in (lo, hi):
            ref = at(me, part)
            ref[...] = ref[...] + full[0, part] + full[1, part]

    ring(lambda i, s: total.at[i, s], p, pl.ds(0, 2), pl.ds(2, 2), half1, full1, to(1, 0), to(-1, 0), r1s, r1r)
    ring(lambda i, s: total.at[p, i, s], q, pl.ds(0, 4), pl.ds(4, 4), half2, full2, to(0, 1), to(0, -1), r2s, r2r)

    def along_z(d):
        return ((y * NZ + (z + d) % NZ) * NX + x, g)

    for d in range(1, NZ):
        send(total.at[p, q, (z + d) % NZ], zgot.at[d - 1], z3s.at[d - 1], z3r.at[d - 1], along_z(d))

    mine.wait()
    every = recvbuf.at[pl.ds(0, CHIPS - 1)]
    got(every, a2r)
    rows = recvbuf[...].astype(F32)
    slots = CHIPS * 8
    tags = jnp.broadcast_to(rows[:, 6:7, :128], (CHIPS, 8, 128)).reshape(slots, 128)
    lane = iota((slots, 128), 1)
    tags = jnp.where((lane >> 4) == (iota((slots, 128), 0) & 7), tags, 0.0).astype(BF16)
    f = iota((128, 128), 0) & 15
    c = iota((128, 128), 1)
    pick = ((f == 0) & (c == 0)) | ((f >= 1) & (f <= 3) & (c == 1)) | ((f >= 4) & (f <= 6) & (c == 2))
    vals = jnp.dot(tags, pick.astype(F32).astype(BF16), preferred_element_type=F32)
    idrow = vals.T[0:1, :]
    selt = (idrow == (iota((8, slots), 0) + 1).astype(F32)).astype(F32)
    sel = (vals[:, 0:1] == (iota((slots, 8), 1) + 1).astype(F32)).astype(F32).astype(BF16)
    cent = jnp.dot(sel, cent_ref[:, :SM], preferred_element_type=F32)
    rows = rows.reshape(slots, SM)
    s256 = lax.rsqrt(jnp.sum(rows * rows, axis=1, keepdims=True) * (1.0 / 256) + EPS)
    small = (rows * s256 - cent).astype(BF16)
    seltb = selt.astype(BF16)
    osums[:, 0:256] = jnp.dot(seltb, small, preferred_element_type=F32)
    osums[:, 256:512] = jnp.dot(seltb, (rows * vals[:, 1:2] - cent).astype(BF16), preferred_element_type=F32)
    osums[:, 512:768] = jnp.dot(seltb, (rows * vals[:, 2:3] - cent).astype(BF16), preferred_element_type=F32)
    osums[:, 768:896] = jnp.broadcast_to(jnp.sum(selt, axis=1, keepdims=True), (8, 128))
    send(osums, psums, pss, psr, partner)
    smallt = small.astype(F32).T

    def gram(c):
        keep = idrow == (c + 1).astype(F32)
        return jnp.dot(jnp.where(keep, smallt, 0.0).astype(BF16), small, preferred_element_type=F32)

    for d in range(1, NZ):
        got(zgot.at[d - 1], z3r.at[d - 1])
    got(psums, psr)
    sums = osums[...] + psums[...]
    count = sums[:, 768:769]
    denom = count + 1.0
    big = total[p, q, z]
    for d in range(1, NZ):
        big = big + zgot[d - 1]
    ca = pl.ds(pl.multiple_of(256 + g * 256, 256), 256)
    cb = pl.ds(pl.multiple_of(256 + g * 512, 256), 256)
    blk[:, 0:256] = ((big[:, :256] - count * cent_ref[:, ca].astype(F32)) / denom).astype(BF16)
    blk[:, 256:512] = ((big[:, 256:] - count * cent_ref[:, cb].astype(F32)) / denom).astype(BF16)
    gf = g.astype(F32)
    part = jnp.where(gf > 0.5, sums[:, 384:768], sums[:, 0:384])
    blk[:, 512:896] = (part / denom).astype(BF16)

    cols = pl.ds(pl.multiple_of(g * HALF, 128), HALF)
    pcols = pl.ds(pl.multiple_of(h * HALF, 128), HALF)

    def chunk(i, j, z0=0, nz=NZ, at=cols):
        yy, xx = (y + 4 + i * g + j * h) % NY, (x + 4 + i * h + j * g) % NX
        return table_ref.at[yy, pl.ds(z0, nz), xx, :, at]

    home = table_ref.at[y, z, x, :, cols]
    for d in range(1, NZ):
        send(blk, home, zs.at[d - 1], zr.at[d - 1], along_z(d))
    own = pltpu.make_async_copy(blk, home, own_sem.at[1])
    own.start()
    for c in range(4):
        pgram[c] = gram(h * 4 + c)
    send(pgram, ogram, pgs, pgr, partner)
    own.wait()
    for d in range(1, NZ):
        got(home, zr.at[d - 1])

    shared = [0]

    def share(i, j):
        k = shared[0]
        shared[0] += 1
        send(chunk(i, j), chunk(i, j), ps.at[k], pr.at[k], partner)

    def ring_out(row, here, plus, minus):
        send(here, here, as_.at[row, 0], ar.at[row, 0], plus)
        send(here, here, as_.at[row, 1], ar.at[row, 1], minus)

    ring_out(0, chunk(0, 0), to(1, 0), to(-1, 0))
    ring_out(1, chunk(0, 0), to(0, 1), to(0, -1))
    share(0, 0)
    for c in range(4):
        gram_ref[c] = gram(g * 4 + c)
    got(chunk(-1, 0), ar.at[0, 0])
    low = chunk(-1, 0, 0, 4)
    send(low, low, as_.at[0, 2], ar.at[0, 2], to(1, 0))
    ring_out(2, chunk(-1, 0), to(0, 1), to(0, -1))
    share(-1, 0)
    got(chunk(1, 0), ar.at[0, 1])
    high = chunk(1, 0, 4, 4)
    send(high, high, as_.at[0, 3], ar.at[0, 3], to(-1, 0))
    ring_out(3, chunk(1, 0), to(0, 1), to(0, -1))
    share(1, 0)

    def second(row, i):
        got(chunk(i, -1), ar.at[row, 0])
        lo = chunk(i, -1, 0, 4)
        send(lo, lo, as_.at[row, 2], ar.at[row, 2], to(0, 1))
        share(i, -1)
        got(chunk(i, 1), ar.at[row, 1])
        hi = chunk(i, 1, 4, 4)
        send(hi, hi, as_.at[row, 3], ar.at[row, 3], to(0, -1))
        share(i, 1)

    second(1, 0)
    got(chunk(2, 0, 0, 4), ar.at[0, 2])
    got(chunk(2, 0, 4, 4), ar.at[0, 3])
    ring_out(4, chunk(2, 0), to(0, 1), to(0, -1))
    share(2, 0)
    second(2, -1)
    second(3, 1)
    second(4, 2)
    got(ogram, pgr)
    for c in range(4):
        one = jnp.sum(jnp.where(iota((8, 1), 0) == g * 4 + c, denom, 0.0), axis=0, keepdims=True)
        gram_ref[c] = (gram_ref[c] + ogram[c]) / one
    for row, i in ((1, 0), (2, -1), (3, 1), (4, 2)):
        got(chunk(i, 2, 0, 4), ar.at[row, 2])
        got(chunk(i, 2, 4, 4), ar.at[row, 3])
        share(i, 2)
    for k in range(16):
        got(chunk(0, 0, at=pcols), pr.at[k])
    got(sendbuf.at[pl.ds(0, CHIPS - 1)], a2s)
    for c in sent:
        c.wait_send()


def route(embeddings, dest, slot, centroids):
    dma = pltpu.SemaphoreType.DMA
    vm = pltpu.VMEM
    n, d = embeddings.shape
    here = pl.BlockSpec(memory_space=pltpu.VMEM)
    return pl.pallas_call(
        routed,
        out_shape=(jax.ShapeDtypeStruct((NY, NZ, NX, 8, WIDE), BF16), jax.ShapeDtypeStruct((4, SM, SM), F32)),
        in_specs=[here] * 4,
        out_specs=(here, here),
        scratch_shapes=[
            vm((CHIPS, 8, SM), BF16), vm((CHIPS, 8, SM), BF16),
            vm((n, d), BF16), vm((n, 1), jnp.int32), vm((n, 1), jnp.int32),
            vm((4, 4, NZ, 8, 512), F32),
            vm((2, 2, NZ, 8, 512), F32), vm((2, 4, NZ, 8, 512), F32),
            vm((2, 4, 8, 512), F32), vm((2, NZ, 8, 512), F32),
            vm((NZ - 1, 8, 512), F32), vm((8, HALF), BF16), vm((8, HALF), F32), vm((8, HALF), F32),
            vm((4, SM, SM), F32), vm((4, SM, SM), F32),
            dma((2,)), dma, dma, dma((3,)), dma((3,)), dma((6,)), dma((6,)), dma((6,)), dma((6,)),
            dma((7,)), dma((7,)), dma, dma, dma, dma,
            dma((7,)), dma((7,)), dma((5, 4)), dma((5, 4)), dma((16,)), dma((16,)),
        ],
        compiler_params=pltpu.CompilerParams(collective_id=1, has_side_effects=True),
        name="routed",
    )(embeddings, dest, slot, centroids)


BLOCKS = (4, 5, 6, 11, 0, 1, 12, 13, 2, 3, 7, 8, 9, 10)


def permuted(lo_map, hi_map, rank_ref, lo_ref, hi_ref, out_ref, hot):
    del lo_map, hi_map

    @pl.when(pl.program_id(0) == 0)
    def _():
        for b in range(8):
            piece = rank_ref[:, b * 128:(b + 1) * 128].astype(F32)
            eye = iota((128, 128), 0) == iota((128, 128), 1)
            col = jnp.sum(jnp.where(eye, piece, 0.0), axis=1, keepdims=True).astype(jnp.int32)
            hot[b * 128:(b + 1) * 128, :] = (iota((128, 1024), 1) == col).astype(F32).astype(BF16)

    both = jnp.concatenate([lo_ref[...], hi_ref[...]], axis=1)
    out_ref[...] = jnp.dot(hot[...], both, preferred_element_type=F32).astype(BF16)


def permute(table, rank):
    k = table.shape[0]
    return pl.pallas_call(
        permuted,
        grid_spec=pltpu.PrefetchScalarGridSpec(
            num_scalar_prefetch=2,
            grid=(7,),
            in_specs=[
                pl.BlockSpec((1, k), lambda j, lo, hi: (0, 0)),
                pl.BlockSpec((k, 128), lambda j, lo, hi: (0, lo[j])),
                pl.BlockSpec((k, 128), lambda j, lo, hi: (0, hi[j])),
            ],
            out_specs=pl.BlockSpec((k, 256), lambda j, lo, hi: (0, j)),
            scratch_shapes=[pltpu.VMEM((k, k), BF16)],
        ),
        out_shape=jax.ShapeDtypeStruct((k, WIDE), BF16),
        name="permuted",
    )(jnp.array(BLOCKS[0::2], jnp.int32), jnp.array(BLOCKS[1::2], jnp.int32), rank, table, table)


def on_device(embeddings, owner_dest, cluster_slot, cluster_rank, centroids):
    table, moment = route(embeddings, owner_dest, cluster_slot, centroids)
    k = cluster_rank.shape[0]
    shift = permute(table.reshape(k, WIDE), cluster_rank.reshape(1, k))
    return (shift, moment)


def solution(mesh):
    placed = (
        P(("dp", "grp"), None),
        P(("dp", "grp"), None),
        P(("dp", "grp"), None),
        P(),
        P("dp", None),
    )
    return jax.shard_map(
        on_device,
        mesh=mesh,
        in_specs=placed,
        out_specs=(P(), P(("dp", "grp"), None, None)),
        check_vma=False,
    )
```

```python
import functools

import jax
import jax.numpy as jnp
from jax import lax
from jax.experimental import pallas as pl
from jax.experimental.pallas import tpu as pltpu
from jax.sharding import PartitionSpec as P

WIDE = 1792
HALF = 896
NX, NY, NZ = 4, 4, 8
CHIPS = 128
SM = 256
MESH = pl.DeviceIdType.MESH
F32 = jnp.float32
BF16 = jnp.bfloat16
EPS = 1e-06


def iota(shape, dim):
    return lax.broadcasted_iota(jnp.int32, shape, dim)


def thirds(v):
    hi = v.astype(BF16)
    rest = v - hi.astype(F32)
    mid = rest.astype(BF16)
    return hi, mid, (rest - mid.astype(F32)).astype(BF16)


def row_of(col):
    n = col.shape[0]
    eye = iota((n, n), 0) == iota((n, n), 1)
    return jnp.sum(jnp.where(eye, col, 0.0), axis=0, keepdims=True)


def col_of(row):
    n = row.shape[1]
    eye = iota((n, n), 0) == iota((n, n), 1)
    return jnp.sum(jnp.where(eye, row, 0.0), axis=1, keepdims=True)


def scales(rows):
    sq = rows * rows
    s512 = jnp.sum(sq[:, :512], axis=1, keepdims=True)
    s1024 = s512 + jnp.sum(sq[:, 512:], axis=1, keepdims=True)
    return lax.rsqrt(s512 * (1.0 / 512) + EPS), lax.rsqrt(s1024 * (1.0 / 1024) + EPS)


def bits(mask):
    return mask.astype(F32).astype(BF16)


def pack(emb_ref, dest, slot, r512, r1024, sendbuf):
    n = dest.shape[1]
    hits = iota((CHIPS, n), 0) == dest
    owner = bits(hits)
    earlier = bits(iota((n, n), 0) < iota((n, n), 1))
    before = jnp.dot(owner, earlier, preferred_element_type=F32)
    pos = jnp.sum(jnp.where(hits, before, 0.0), axis=0, keepdims=True).astype(jnp.int32)
    values = [slot.astype(F32) + 1.0]
    for s in (r512, r1024):
        values += [t.astype(F32) for t in thirds(s)]
    line = iota((128, n), 0)
    tags = jnp.zeros((128, n), F32)
    for i, v in enumerate(values):
        tags = jnp.where((line & 15) == i, v, tags)
    tags = jnp.where((line >> 4) == pos, tags, 0.0).astype(BF16)
    tags = lax.dot_general(owner, tags, (((1,), (1,)), ((), ())), preferred_element_type=F32)
    place = bits(iota((CHIPS * 8, n), 0) == dest * 8 + pos)
    rows = jnp.dot(place, emb_ref[:, :SM], preferred_element_type=F32).reshape(CHIPS, 8, SM)
    wide = jnp.concatenate([tags, jnp.zeros((CHIPS, SM - 128), F32)], axis=1)
    rows = jnp.where(iota((CHIPS, 8, SM), 1) == 6, wide[:, None, :], rows)
    sendbuf[...] = rows.astype(BF16)


def order_of(dest, slot, g):
    xx, zz, yy = dest & 3, (dest >> 2) & 7, dest >> 5
    a = xx * (1 - g) + yy * g
    b = yy * (1 - g) + xx * g
    return ((a * 4 + b) * 8 + zz) * 8 + slot


def columns(g):
    return (pl.ds(pl.multiple_of(256 + g * 256, 256), 256), pl.ds(pl.multiple_of(256 + g * 512, 256), 256))


def whole(order, xs, ss, total, add):
    k = 8 * CHIPS
    hot = bits(iota((k, order.shape[1]), 0) == order)
    for at, x, s in zip((0, 256), xs, ss):
        acc = None
        for t in thirds(x.astype(F32) * s):
            part = jnp.dot(hot, t, preferred_element_type=F32)
            acc = part if acc is None else acc + part
        acc = acc.reshape(4, 4, NZ, 8, 256)
        if add:
            acc = acc + total[:, :, :, :, at:at + 256]
        total[:, :, :, :, at:at + 256] = acc


def routed(emb_ref, dest_ref, slot_ref, cent_ref, table_ref, gram_ref,
           sendbuf, recvbuf, pxa, pxb, info, pinfo, total, half1, full1, half2, full2, zgot, blk, psums, osums,
           pgram, ogram,
           own_sem, a2s, a2r, xs, xr, r1s, r1r, r2s, r2r, z3s, z3r, pss, psr, pgs, pgr,
           zs, zr, as_, ar, ps, pr):
    dp = lax.axis_index("dp")
    g = lax.axis_index("grp")
    x = dp % NX
    z = (dp // NX) % NZ
    y = dp // (NX * NZ)
    h = 1 - g
    partner = (dp, h)
    barrier = pltpu.get_barrier_semaphore()
    pl.semaphore_signal(barrier, inc=1, device_id=partner, device_id_type=MESH)

    def chip(d):
        return (((y + 2 + d // 32) % NY) * NZ + (z + 4 + (d // 4) % NZ) % NZ) * NX + (x + 2 + d % 4) % NX

    def others(body):
        lax.fori_loop(0, 82, body, 0)
        lax.fori_loop(83, CHIPS, body, 0)

    def greet(d, c):
        pl.semaphore_signal(barrier, inc=1, device_id=(chip(d), g), device_id_type=MESH)
        return c

    others(greet)
    dest, slot = dest_ref[...], slot_ref[...]
    c512, c1024 = scales(emb_ref[...].astype(F32))
    r512, r1024 = row_of(c512), row_of(c1024)
    gf = g.astype(F32)
    info[...] = jnp.zeros_like(info)
    info[0:1, :] = order_of(dest, slot, h).astype(F32)
    info[1:2, :] = r512 * gf + r1024 * (1.0 - gf)
    info[2:3, :] = r1024
    ca, cb = columns(g)
    whole(order_of(dest, slot, g), (emb_ref[:, ca], emb_ref[:, cb]), (c512 * (1.0 - gf) + c1024 * gf, c1024), total, False)
    pl.semaphore_wait(barrier, CHIPS)

    sent = []

    def send(src, dst, ss, rs, peer):
        c = pltpu.make_async_remote_copy(src_ref=src, dst_ref=dst, send_sem=ss, recv_sem=rs,
                                         device_id=peer, device_id_type=MESH)
        c.start()
        sent.append(c)

    def got(ref, sem):
        pltpu.make_async_copy(ref, ref, sem).wait()

    pa, pb = columns(h)
    send(info, pinfo, xs.at[0], xr.at[0], partner)
    send(emb_ref.at[:, pa], pxa, xs.at[1], xr.at[1], partner)
    send(emb_ref.at[:, pb], pxb, xs.at[2], xr.at[2], partner)
    pack(emb_ref, dest, slot, r512, r1024, sendbuf)
    mine = pltpu.make_async_copy(sendbuf.at[dp], recvbuf.at[dp], own_sem.at[0])
    mine.start()
    got(pinfo, xr.at[0])
    got(pxa, xr.at[1])
    got(pxb, xr.at[2])
    whole(pinfo[0:1, :].astype(jnp.int32), (pxa[...], pxb[...]), (col_of(pinfo[1:2, :]), col_of(pinfo[2:3, :])), total, True)

    def scatter(d, c):
        t = chip(d)
        pltpu.make_async_remote_copy(src_ref=sendbuf.at[t], dst_ref=recvbuf.at[dp], send_sem=a2s, recv_sem=a2r,
                                     device_id=(t, g), device_id_type=MESH).start()
        return c

    def to(i, j):
        yy, xx = (y + 4 + i * g + j * h) % NY, (x + 4 + i * h + j * g) % NX
        return ((yy * NZ + z) * NX + xx, g)

    p = x * h + y * g
    q = y * h + x * g

    def ring(at, me, lo, hi, half, full, plus, minus, ss, rs, between):
        up, down, far = (me + 1) % 4, (me + 3) % 4, (me + 2) % 4
        send(at(far, lo), half.at[0], ss.at[0], rs.at[0], plus)
        send(at(far, hi), half.at[1], ss.at[1], rs.at[1], minus)
        send(at(up, hi), full.at[0, hi], ss.at[2], rs.at[2], plus)
        send(at(down, lo), full.at[1, lo], ss.at[3], rs.at[3], minus)
        between()
        got(half.at[0], rs.at[0])
        ref = at(up, lo)
        ref[...] = ref[...] + half[0]
        send(ref, full.at[0, lo], ss.at[4], rs.at[4], plus)
        got(half.at[1], rs.at[1])
        ref = at(down, hi)
        ref[...] = ref[...] + half[1]
        send(ref, full.at[1, hi], ss.at[5], rs.at[5], minus)
        got(full.at[0, hi], rs.at[2])
        got(full.at[1, lo], rs.at[3])
        got(full.at[0, lo], rs.at[4])
        got(full.at[1, hi], rs.at[5])
        for part in (lo, hi):
            ref = at(me, part)
            ref[...] = ref[...] + full[0, part] + full[1, part]

    ring(lambda i, s: total.at[i, s], p, pl.ds(0, 2), pl.ds(2, 2), half1, full1, to(1, 0), to(-1, 0), r1s, r1r,
         lambda: others(scatter))
    ring(lambda i, s: total.at[p, i, s], q, pl.ds(0, 4), pl.ds(4, 4), half2, full2, to(0, 1), to(0, -1), r2s, r2r,
         lambda: None)

    def along_z(d):
        return ((y * NZ + (z + d) % NZ) * NX + x, g)

    for d in range(1, NZ):
        send(total.at[p, q, (z + d) % NZ], zgot.at[d - 1], z3s.at[d - 1], z3r.at[d - 1], along_z(d))

    mine.wait()
    every = recvbuf.at[pl.ds(0, CHIPS - 1)]
    got(every, a2r)
    rows = recvbuf[...].astype(F32)
    slots = CHIPS * 8
    tags = jnp.broadcast_to(rows[:, 6:7, :128], (CHIPS, 8, 128)).reshape(slots, 128)
    lane = iota((slots, 128), 1)
    tags = jnp.where((lane >> 4) == (iota((slots, 128), 0) & 7), tags, 0.0).astype(BF16)
    f = iota((128, 128), 0) & 15
    c = iota((128, 128), 1)
    pick = ((f == 0) & (c == 0)) | ((f >= 1) & (f <= 3) & (c == 1)) | ((f >= 4) & (f <= 6) & (c == 2))
    vals = jnp.dot(tags, pick.astype(F32).astype(BF16), preferred_element_type=F32)
    idrow = vals.T[0:1, :]
    selt = (idrow == (iota((8, slots), 0) + 1).astype(F32)).astype(F32)
    sel = (vals[:, 0:1] == (iota((slots, 8), 1) + 1).astype(F32)).astype(F32).astype(BF16)
    cent = jnp.dot(sel, cent_ref[:, :SM], preferred_element_type=F32)
    rows = rows.reshape(slots, SM)
    s256 = lax.rsqrt(jnp.sum(rows * rows, axis=1, keepdims=True) * (1.0 / 256) + EPS)
    small = (rows * s256 - cent).astype(BF16)
    seltb = selt.astype(BF16)
    osums[:, 0:256] = jnp.dot(seltb, small, preferred_element_type=F32)
    osums[:, 256:512] = jnp.dot(seltb, (rows * vals[:, 1:2] - cent).astype(BF16), preferred_element_type=F32)
    osums[:, 512:768] = jnp.dot(seltb, (rows * vals[:, 2:3] - cent).astype(BF16), preferred_element_type=F32)
    osums[:, 768:896] = jnp.broadcast_to(jnp.sum(selt, axis=1, keepdims=True), (8, 128))
    send(osums, psums, pss, psr, partner)
    smallt = small.astype(F32).T

    def gram(c):
        keep = idrow == (c + 1).astype(F32)
        return jnp.dot(jnp.where(keep, smallt, 0.0).astype(BF16), small, preferred_element_type=F32)

    for d in range(1, NZ):
        got(zgot.at[d - 1], z3r.at[d - 1])
    got(psums, psr)
    sums = osums[...] + psums[...]
    count = sums[:, 768:769]
    denom = count + 1.0
    big = total[p, q, z]
    for d in range(1, NZ):
        big = big + zgot[d - 1]
    blk[:, 0:256] = ((big[:, :256] - count * cent_ref[:, ca].astype(F32)) / denom).astype(BF16)
    blk[:, 256:512] = ((big[:, 256:] - count * cent_ref[:, cb].astype(F32)) / denom).astype(BF16)
    part = jnp.where(gf > 0.5, sums[:, 384:768], sums[:, 0:384])
    blk[:, 512:896] = (part / denom).astype(BF16)

    cols = pl.ds(pl.multiple_of(g * HALF, 128), HALF)
    pcols = pl.ds(pl.multiple_of(h * HALF, 128), HALF)

    def chunk(i, j, z0=0, nz=NZ, at=cols):
        yy, xx = (y + 4 + i * g + j * h) % NY, (x + 4 + i * h + j * g) % NX
        return table_ref.at[yy, pl.ds(z0, nz), xx, :, at]

    home = table_ref.at[y, z, x, :, cols]
    for d in range(1, NZ):
        send(blk, home, zs.at[d - 1], zr.at[d - 1], along_z(d))
    own = pltpu.make_async_copy(blk, home, own_sem.at[1])
    own.start()
    for c in range(4):
        pgram[c] = gram(h * 4 + c)
    send(pgram, ogram, pgs, pgr, partner)
    own.wait()
    for d in range(1, NZ):
        got(home, zr.at[d - 1])

    shared = [0]

    def share(i, j):
        k = shared[0]
        shared[0] += 1
        send(chunk(i, j), chunk(i, j), ps.at[k], pr.at[k], partner)

    def ring_out(row, here, plus, minus):
        send(here, here, as_.at[row, 0], ar.at[row, 0], plus)
        send(here, here, as_.at[row, 1], ar.at[row, 1], minus)

    ring_out(0, chunk(0, 0), to(1, 0), to(-1, 0))
    ring_out(1, chunk(0, 0), to(0, 1), to(0, -1))
    share(0, 0)
    for c in range(4):
        gram_ref[c] = gram(g * 4 + c)
    got(chunk(-1, 0), ar.at[0, 0])
    low = chunk(-1, 0, 0, 4)
    send(low, low, as_.at[0, 2], ar.at[0, 2], to(1, 0))
    ring_out(2, chunk(-1, 0), to(0, 1), to(0, -1))
    share(-1, 0)
    got(chunk(1, 0), ar.at[0, 1])
    high = chunk(1, 0, 4, 4)
    send(high, high, as_.at[0, 3], ar.at[0, 3], to(-1, 0))
    ring_out(3, chunk(1, 0), to(0, 1), to(0, -1))
    share(1, 0)

    def second(row, i):
        got(chunk(i, -1), ar.at[row, 0])
        lo = chunk(i, -1, 0, 4)
        send(lo, lo, as_.at[row, 2], ar.at[row, 2], to(0, 1))
        share(i, -1)
        got(chunk(i, 1), ar.at[row, 1])
        hi = chunk(i, 1, 4, 4)
        send(hi, hi, as_.at[row, 3], ar.at[row, 3], to(0, -1))
        share(i, 1)

    second(1, 0)
    got(chunk(2, 0, 0, 4), ar.at[0, 2])
    got(chunk(2, 0, 4, 4), ar.at[0, 3])
    ring_out(4, chunk(2, 0), to(0, 1), to(0, -1))
    share(2, 0)
    second(2, -1)
    second(3, 1)
    second(4, 2)
    got(ogram, pgr)
    for c in range(4):
        one = jnp.sum(jnp.where(iota((8, 1), 0) == g * 4 + c, denom, 0.0), axis=0, keepdims=True)
        gram_ref[c] = (gram_ref[c] + ogram[c]) / one
    for row, i in ((1, 0), (2, -1), (3, 1), (4, 2)):
        got(chunk(i, 2, 0, 4), ar.at[row, 2])
        got(chunk(i, 2, 4, 4), ar.at[row, 3])
        share(i, 2)
    for k in range(16):
        got(chunk(0, 0, at=pcols), pr.at[k])
    got(sendbuf.at[pl.ds(0, CHIPS - 1)], a2s)
    for c in sent:
        c.wait_send()


def route(embeddings, dest, slot, centroids):
    dma = pltpu.SemaphoreType.DMA
    vm = pltpu.VMEM
    n = embeddings.shape[0]
    here = pl.BlockSpec(memory_space=pltpu.VMEM)
    return pl.pallas_call(
        routed,
        out_shape=(jax.ShapeDtypeStruct((NY, NZ, NX, 8, WIDE), BF16), jax.ShapeDtypeStruct((4, SM, SM), F32)),
        in_specs=[here] * 4,
        out_specs=(here, here),
        scratch_shapes=[
            vm((CHIPS, 8, SM), BF16), vm((CHIPS, 8, SM), BF16),
            vm((n, 256), BF16), vm((n, 256), BF16), vm((8, n), F32), vm((8, n), F32),
            vm((4, 4, NZ, 8, 512), F32),
            vm((2, 2, NZ, 8, 512), F32), vm((2, 4, NZ, 8, 512), F32),
            vm((2, 4, 8, 512), F32), vm((2, NZ, 8, 512), F32),
            vm((NZ - 1, 8, 512), F32), vm((8, HALF), BF16), vm((8, HALF), F32), vm((8, HALF), F32),
            vm((4, SM, SM), F32), vm((4, SM, SM), F32),
            dma((2,)), dma, dma, dma((3,)), dma((3,)), dma((6,)), dma((6,)), dma((6,)), dma((6,)),
            dma((7,)), dma((7,)), dma, dma, dma, dma,
            dma((7,)), dma((7,)), dma((5, 4)), dma((5, 4)), dma((16,)), dma((16,)),
        ],
        compiler_params=pltpu.CompilerParams(collective_id=1, has_side_effects=True),
        name="routed",
    )(embeddings, dest, slot, centroids)


BLOCKS = (4, 5, 6, 11, 0, 1, 12, 13, 2, 3, 7, 8, 9, 10)


def permuted(lo_map, hi_map, rank_ref, lo_ref, hi_ref, gram_ref, out_ref, moment_ref, hot):
    del lo_map, hi_map

    @pl.when(pl.program_id(0) == 0)
    def _():
        for b in range(8):
            piece = rank_ref[:, b * 128:(b + 1) * 128].astype(F32)
            eye = iota((128, 128), 0) == iota((128, 128), 1)
            col = jnp.sum(jnp.where(eye, piece, 0.0), axis=1, keepdims=True).astype(jnp.int32)
            hot[b * 128:(b + 1) * 128, :] = (iota((128, 1024), 1) == col).astype(F32).astype(BF16)

    @pl.when(pl.program_id(0) < 4)
    def _():
        moment_ref[...] = gram_ref[...]

    both = jnp.concatenate([lo_ref[...], hi_ref[...]], axis=1)
    out_ref[...] = jnp.dot(hot[...], both, preferred_element_type=F32).astype(BF16)


def permute(table, rank, gram):
    k = table.shape[0]
    return pl.pallas_call(
        permuted,
        grid_spec=pltpu.PrefetchScalarGridSpec(
            num_scalar_prefetch=2,
            grid=(7,),
            in_specs=[
                pl.BlockSpec((1, k), lambda j, lo, hi: (0, 0)),
                pl.BlockSpec((k, 128), lambda j, lo, hi: (0, lo[j])),
                pl.BlockSpec((k, 128), lambda j, lo, hi: (0, hi[j])),
                pl.BlockSpec((1, SM, SM), lambda j, lo, hi: (jnp.minimum(j, 3), 0, 0)),
            ],
            out_specs=(
                pl.BlockSpec((k, 256), lambda j, lo, hi: (0, j)),
                pl.BlockSpec((1, SM, SM), lambda j, lo, hi: (jnp.minimum(j, 3), 0, 0)),
            ),
            scratch_shapes=[pltpu.VMEM((k, k), BF16)],
        ),
        out_shape=(jax.ShapeDtypeStruct((k, WIDE), BF16), jax.ShapeDtypeStruct(gram.shape, F32)),
        name="permuted",
    )(jnp.array(BLOCKS[0::2], jnp.int32), jnp.array(BLOCKS[1::2], jnp.int32), rank, table, table, gram)


def on_device(embeddings, owner_dest, cluster_slot, cluster_rank, centroids):
    n = embeddings.shape[0]
    table, gram = route(embeddings, owner_dest.reshape(1, n), cluster_slot.reshape(1, n), centroids)
    k = cluster_rank.shape[0]
    return permute(table.reshape(k, WIDE), cluster_rank.reshape(1, k), gram)


def solution(mesh):
    placed = (
        P(("dp", "grp"), None),
        P(("dp", "grp"), None),
        P(("dp", "grp"), None),
        P(),
        P("dp", None),
    )
    return jax.shard_map(
        on_device,
        mesh=mesh,
        in_specs=placed,
        out_specs=(P(), P(("dp", "grp"), None, None)),
        check_vma=False,
    )
```

```python
import functools

import jax
import jax.numpy as jnp
from jax import lax
from jax.experimental import pallas as pl
from jax.experimental.pallas import tpu as pltpu
from jax.sharding import PartitionSpec as P

WIDE = 1792
HALF = 896
NX, NY, NZ = 4, 4, 8
CHIPS = 128
SM = 256
MESH = pl.DeviceIdType.MESH
F32 = jnp.float32
BF16 = jnp.bfloat16
EPS = 1e-06


def iota(shape, dim):
    return lax.broadcasted_iota(jnp.int32, shape, dim)


def thirds(v):
    hi = v.astype(BF16)
    rest = v - hi.astype(F32)
    mid = rest.astype(BF16)
    return hi, mid, (rest - mid.astype(F32)).astype(BF16)


def row_of(col):
    n = col.shape[0]
    eye = iota((n, n), 0) == iota((n, n), 1)
    return jnp.sum(jnp.where(eye, col, 0.0), axis=0, keepdims=True)


def col_of(row):
    n = row.shape[1]
    eye = iota((n, n), 0) == iota((n, n), 1)
    return jnp.sum(jnp.where(eye, row, 0.0), axis=1, keepdims=True)


def scales(rows):
    sq = rows * rows
    s512 = jnp.sum(sq[:, :512], axis=1, keepdims=True)
    s1024 = s512 + jnp.sum(sq[:, 512:], axis=1, keepdims=True)
    return lax.rsqrt(s512 * (1.0 / 512) + EPS), lax.rsqrt(s1024 * (1.0 / 1024) + EPS)


def bits(mask):
    return mask.astype(F32).astype(BF16)


def pack(emb_ref, dest, slot, r512, r1024, sendbuf):
    n = dest.shape[1]
    hits = iota((CHIPS, n), 0) == dest
    owner = bits(hits)
    earlier = bits(iota((n, n), 0) < iota((n, n), 1))
    before = jnp.dot(owner, earlier, preferred_element_type=F32)
    pos = jnp.sum(jnp.where(hits, before, 0.0), axis=0, keepdims=True).astype(jnp.int32)
    values = [slot.astype(F32) + 1.0]
    for s in (r512, r1024):
        values += [t.astype(F32) for t in thirds(s)]
    line = iota((128, n), 0)
    tags = jnp.zeros((128, n), F32)
    for i, v in enumerate(values):
        tags = jnp.where((line & 15) == i, v, tags)
    tags = jnp.where((line >> 4) == pos, tags, 0.0).astype(BF16)
    tags = lax.dot_general(owner, tags, (((1,), (1,)), ((), ())), preferred_element_type=F32)
    place = bits(iota((CHIPS * 8, n), 0) == dest * 8 + pos)
    rows = jnp.dot(place, emb_ref[:, :SM], preferred_element_type=F32).reshape(CHIPS, 8, SM)
    wide = jnp.concatenate([tags, jnp.zeros((CHIPS, SM - 128), F32)], axis=1)
    rows = jnp.where(iota((CHIPS, 8, SM), 1) == 6, wide[:, None, :], rows)
    sendbuf[...] = rows.astype(BF16)


def order_of(dest, slot, g):
    xx, zz, yy = dest & 3, (dest >> 2) & 7, dest >> 5
    a = xx * (1 - g) + yy * g
    b = yy * (1 - g) + xx * g
    return ((a * 4 + b) * 8 + zz) * 8 + slot


def columns(g):
    return (pl.ds(pl.multiple_of(256 + g * 256, 256), 256), pl.ds(pl.multiple_of(256 + g * 512, 256), 256))


def whole(order, xs, ss, total, add):
    k = 8 * CHIPS
    hot = bits(iota((k, order.shape[1]), 0) == order)
    for at, x, s in zip((0, 256), xs, ss):
        acc = None
        for t in thirds(x.astype(F32) * s):
            part = jnp.dot(hot, t, preferred_element_type=F32)
            acc = part if acc is None else acc + part
        acc = acc.reshape(4, 4, NZ, 8, 256)
        if add:
            acc = acc + total[:, :, :, :, at:at + 256]
        total[:, :, :, :, at:at + 256] = acc


def routed(emb_ref, dest_ref, slot_ref, cent_ref, rank_ref, table_out, gram_out, hot_out, table_ref, gram_ref, hot_ref,
           sendbuf, recvbuf, pxa, pxb, info, pinfo, total, half1, full1, full2, zgot, blk, psums, osums,
           pgram, ogram,
           own_sem, a2s, a2r, xs, xr, r1s, r1r, r2s, r2r, z3s, z3r, pss, psr, pgs, pgr,
           zs, zr, as_, ar, ps, pr, outs):
    dp = lax.axis_index("dp")
    g = lax.axis_index("grp")
    x = dp % NX
    z = (dp // NX) % NZ
    y = dp // (NX * NZ)
    h = 1 - g
    partner = (dp, h)
    barrier = pltpu.get_barrier_semaphore()
    pl.semaphore_signal(barrier, inc=1, device_id=partner, device_id_type=MESH)

    def chip(d):
        return (((y + 2 + d // 32) % NY) * NZ + (z + 4 + (d // 4) % NZ) % NZ) * NX + (x + 2 + d % 4) % NX

    def others(body):
        lax.fori_loop(0, 82, body, 0)
        lax.fori_loop(83, CHIPS, body, 0)

    def greet(d, c):
        pl.semaphore_signal(barrier, inc=1, device_id=(chip(d), g), device_id_type=MESH)
        return c

    others(greet)
    dest, slot = dest_ref[...], slot_ref[...]
    c512, c1024 = scales(emb_ref[...].astype(F32))
    r512, r1024 = row_of(c512), row_of(c1024)
    gf = g.astype(F32)
    info[...] = jnp.zeros_like(info)
    info[0:1, :] = order_of(dest, slot, h).astype(F32)
    info[1:2, :] = r512 * gf + r1024 * (1.0 - gf)
    info[2:3, :] = r1024
    ca, cb = columns(g)
    whole(order_of(dest, slot, g), (emb_ref[:, ca], emb_ref[:, cb]), (c512 * (1.0 - gf) + c1024 * gf, c1024), total, False)
    pl.semaphore_wait(barrier, CHIPS)

    sent = []

    def send(src, dst, ss, rs, peer):
        c = pltpu.make_async_remote_copy(src_ref=src, dst_ref=dst, send_sem=ss, recv_sem=rs,
                                         device_id=peer, device_id_type=MESH)
        c.start()
        sent.append(c)

    def got(ref, sem):
        pltpu.make_async_copy(ref, ref, sem).wait()

    pa, pb = columns(h)
    send(info, pinfo, xs.at[0], xr.at[0], partner)
    send(emb_ref.at[:, pa], pxa, xs.at[1], xr.at[1], partner)
    send(emb_ref.at[:, pb], pxb, xs.at[2], xr.at[2], partner)
    pack(emb_ref, dest, slot, r512, r1024, sendbuf)
    mine = pltpu.make_async_copy(sendbuf.at[dp], recvbuf.at[dp], own_sem.at[0])
    mine.start()
    got(pinfo, xr.at[0])
    got(pxa, xr.at[1])
    got(pxb, xr.at[2])
    whole(pinfo[0:1, :].astype(jnp.int32), (pxa[...], pxb[...]), (col_of(pinfo[1:2, :]), col_of(pinfo[2:3, :])), total, True)

    def scatter(d, c):
        t = chip(d)
        pltpu.make_async_remote_copy(src_ref=sendbuf.at[t], dst_ref=recvbuf.at[dp], send_sem=a2s, recv_sem=a2r,
                                     device_id=(t, g), device_id_type=MESH).start()
        return c

    def to(i, j):
        yy, xx = (y + 4 + i * g + j * h) % NY, (x + 4 + i * h + j * g) % NX
        return ((yy * NZ + z) * NX + xx, g)

    p = x * h + y * g
    q = y * h + x * g

    def ring(at, me, lo, hi, half, full, plus, minus, ss, rs, between):
        up, down, far = (me + 1) % 4, (me + 3) % 4, (me + 2) % 4
        send(at(far, lo), half.at[0], ss.at[0], rs.at[0], plus)
        send(at(far, hi), half.at[1], ss.at[1], rs.at[1], minus)
        send(at(up, hi), full.at[0, hi], ss.at[2], rs.at[2], plus)
        send(at(down, lo), full.at[1, lo], ss.at[3], rs.at[3], minus)
        got(half.at[0], rs.at[0])
        ref = at(up, lo)
        ref[...] = ref[...] + half[0]
        send(ref, full.at[0, lo], ss.at[4], rs.at[4], plus)
        got(half.at[1], rs.at[1])
        ref = at(down, hi)
        ref[...] = ref[...] + half[1]
        send(ref, full.at[1, hi], ss.at[5], rs.at[5], minus)
        between()
        got(full.at[0, hi], rs.at[2])
        got(full.at[1, lo], rs.at[3])
        got(full.at[0, lo], rs.at[4])
        got(full.at[1, hi], rs.at[5])
        for part in (lo, hi):
            ref = at(me, part)
            ref[...] = ref[...] + full[0, part] + full[1, part]

    ring(lambda i, s: total.at[i, s], p, pl.ds(0, 2), pl.ds(2, 2), half1, full1, to(1, 0), to(-1, 0), r1s, r1r,
         lambda: others(scatter))
    for i in (2, 1, 3):
        send(total.at[p, (q + i) % 4], full2.at[i - 1], r2s.at[i - 1], r2r.at[i - 1], to(0, i))
    for i in (1, 3, 2):
        got(full2.at[i - 1], r2r.at[i - 1])
    total[p, q] = total[p, q] + full2[0] + full2[1] + full2[2]

    def along_z(d):
        return ((y * NZ + (z + d) % NZ) * NX + x, g)

    for d in range(1, NZ):
        send(total.at[p, q, (z + d) % NZ], zgot.at[d - 1], z3s.at[d - 1], z3r.at[d - 1], along_z(d))

    mine.wait()
    every = recvbuf.at[pl.ds(0, CHIPS - 1)]
    got(every, a2r)
    rows = recvbuf[...].astype(F32)
    slots = CHIPS * 8
    tags = jnp.broadcast_to(rows[:, 6:7, :128], (CHIPS, 8, 128)).reshape(slots, 128)
    lane = iota((slots, 128), 1)
    tags = jnp.where((lane >> 4) == (iota((slots, 128), 0) & 7), tags, 0.0).astype(BF16)
    f = iota((128, 128), 0) & 15
    c = iota((128, 128), 1)
    pick = ((f == 0) & (c == 0)) | ((f >= 1) & (f <= 3) & (c == 1)) | ((f >= 4) & (f <= 6) & (c == 2))
    vals = jnp.dot(tags, pick.astype(F32).astype(BF16), preferred_element_type=F32)
    idrow = vals.T[0:1, :]
    selt = (idrow == (iota((8, slots), 0) + 1).astype(F32)).astype(F32)
    sel = (vals[:, 0:1] == (iota((slots, 8), 1) + 1).astype(F32)).astype(F32).astype(BF16)
    cent = jnp.dot(sel, cent_ref[:, :SM], preferred_element_type=F32)
    rows = rows.reshape(slots, SM)
    s256 = lax.rsqrt(jnp.sum(rows * rows, axis=1, keepdims=True) * (1.0 / 256) + EPS)
    small = (rows * s256 - cent).astype(BF16)
    seltb = selt.astype(BF16)
    osums[:, 0:256] = jnp.dot(seltb, small, preferred_element_type=F32)
    osums[:, 256:512] = jnp.dot(seltb, (rows * vals[:, 1:2] - cent).astype(BF16), preferred_element_type=F32)
    osums[:, 512:768] = jnp.dot(seltb, (rows * vals[:, 2:3] - cent).astype(BF16), preferred_element_type=F32)
    osums[:, 768:896] = jnp.broadcast_to(jnp.sum(selt, axis=1, keepdims=True), (8, 128))
    send(osums, psums, pss, psr, partner)
    smallt = small.astype(F32).T

    def gram(c):
        keep = idrow == (c + 1).astype(F32)
        return jnp.dot(jnp.where(keep, smallt, 0.0).astype(BF16), small, preferred_element_type=F32)

    for d in range(1, NZ):
        got(zgot.at[d - 1], z3r.at[d - 1])
    got(psums, psr)
    sums = osums[...] + psums[...]
    count = sums[:, 768:769]
    denom = count + 1.0
    big = total[p, q, z]
    for d in range(1, NZ):
        big = big + zgot[d - 1]
    blk[:, 0:256] = ((big[:, :256] - count * cent_ref[:, ca].astype(F32)) / denom).astype(BF16)
    blk[:, 256:512] = ((big[:, 256:] - count * cent_ref[:, cb].astype(F32)) / denom).astype(BF16)
    part = jnp.where(gf > 0.5, sums[:, 384:768], sums[:, 0:384])
    blk[:, 512:896] = (part / denom).astype(BF16)

    cols = pl.ds(pl.multiple_of(g * HALF, 128), HALF)
    pcols = pl.ds(pl.multiple_of(h * HALF, 128), HALF)

    def chunk(i, j, z0=0, nz=NZ, at=cols):
        yy, xx = (y + 4 + i * g + j * h) % NY, (x + 4 + i * h + j * g) % NX
        return table_ref.at[yy, pl.ds(z0, nz), xx, :, at]

    home = table_ref.at[y, z, x, :, cols]
    for d in range(1, NZ):
        send(blk, home, zs.at[d - 1], zr.at[d - 1], along_z(d))
    own = pltpu.make_async_copy(blk, home, own_sem.at[1])
    own.start()
    for c in range(4):
        pgram[c] = gram(h * 4 + c)
    send(pgram, ogram, pgs, pgr, partner)
    for b in range(8):
        piece = rank_ref[:, b * 128:(b + 1) * 128].astype(F32)
        col = col_of(piece).astype(jnp.int32)
        hot_ref[b * 128:(b + 1) * 128, :] = bits(iota((128, 1024), 1) == col)
    hot_copy = pltpu.make_async_copy(hot_ref, hot_out, outs.at[0])
    hot_copy.start()
    own.wait()
    for d in range(1, NZ):
        got(home, zr.at[d - 1])

    seen = []

    def keep(yy, xx, at):
        pltpu.make_async_copy(table_ref.at[yy, :, xx, :, at], table_out.at[yy, :, xx, :, at], outs.at[1]).start()

    def take(k):
        i, j = seen[k]
        yy, xx = (y + 4 + i * h + j * g) % NY, (x + 4 + i * g + j * h) % NX
        got(table_ref.at[yy, :, xx, :, pcols], pr.at[k])
        keep(yy, xx, pcols)

    def share(i, j):
        k = len(seen)
        seen.append((i, j))
        send(chunk(i, j), chunk(i, j), ps.at[k], pr.at[k], partner)
        keep((y + 4 + i * g + j * h) % NY, (x + 4 + i * h + j * g) % NX, cols)
        if k >= 5:
            take(k - 5)

    def out(row, here, along, far):
        send(here, here, as_.at[row, 0], ar.at[row, 0], along(1))
        send(here, here, as_.at[row, 1], ar.at[row, 1], along(-1))
        if far:
            send(here, here, as_.at[row, 2], ar.at[row, 2], along(2))

    def first(i):
        return to(i, 0)

    def second(i):
        return to(0, i)

    out(0, chunk(0, 0), first, True)
    out(1, chunk(0, 0), second, False)
    share(0, 0)
    for c in range(4):
        gram_ref[c] = gram(g * 4 + c)
    got(chunk(-1, 0), ar.at[0, 0])
    out(2, chunk(-1, 0), second, False)
    got(chunk(1, 0), ar.at[0, 1])
    out(3, chunk(1, 0), second, False)
    share(-1, 0)
    share(1, 0)

    def pass_on(row, i):
        got(chunk(i, -1), ar.at[row, 0])
        lo = chunk(i, -1, 0, 4)
        send(lo, lo, as_.at[row, 2], ar.at[row, 2], to(0, 1))
        got(chunk(i, 1), ar.at[row, 1])
        hi = chunk(i, 1, 4, 4)
        send(hi, hi, as_.at[row, 3], ar.at[row, 3], to(0, -1))
        share(i, -1)
        share(i, 1)

    pass_on(1, 0)
    got(chunk(2, 0), ar.at[0, 2])
    out(4, chunk(2, 0), second, True)
    share(2, 0)
    pass_on(2, -1)
    pass_on(3, 1)
    got(ogram, pgr)
    for c in range(4):
        one = jnp.sum(jnp.where(iota((8, 1), 0) == g * 4 + c, denom, 0.0), axis=0, keepdims=True)
        gram_ref[c] = (gram_ref[c] + ogram[c]) / one
    gram_copy = pltpu.make_async_copy(gram_ref, gram_out, outs.at[2])
    gram_copy.start()
    for row, i in ((1, 0), (2, -1), (3, 1)):
        got(chunk(i, 2, 0, 4), ar.at[row, 2])
        got(chunk(i, 2, 4, 4), ar.at[row, 3])
        share(i, 2)
    for n, i in enumerate((-1, 1, 2)):
        got(chunk(2, i), ar.at[4, n])
        share(2, i)
    for k in range(11, 16):
        take(k)
    hot_copy.wait()
    gram_copy.wait()
    pltpu.make_async_copy(table_ref, table_out, outs.at[1]).wait()
    got(sendbuf.at[pl.ds(0, CHIPS - 1)], a2s)
    for c in sent:
        c.wait_send()


def route(embeddings, dest, slot, centroids, rank):
    dma = pltpu.SemaphoreType.DMA
    vm = pltpu.VMEM
    n = embeddings.shape[0]
    here = pl.BlockSpec(memory_space=pltpu.VMEM)
    return pl.pallas_call(
        routed,
        out_shape=(jax.ShapeDtypeStruct((NY, NZ, NX, 8, WIDE), BF16), jax.ShapeDtypeStruct((4, SM, SM), F32),
                   jax.ShapeDtypeStruct((1024, 1024), BF16)),
        in_specs=[here] * 5,
        out_specs=(pl.BlockSpec(memory_space=pl.ANY),) * 3,
        scratch_shapes=[
            vm((NY, NZ, NX, 8, WIDE), BF16), vm((4, SM, SM), F32), vm((1024, 1024), BF16),
            vm((CHIPS, 8, SM), BF16), vm((CHIPS, 8, SM), BF16),
            vm((n, 256), BF16), vm((n, 256), BF16), vm((8, n), F32), vm((8, n), F32),
            vm((4, 4, NZ, 8, 512), F32),
            vm((2, 2, NZ, 8, 512), F32), vm((2, 4, NZ, 8, 512), F32),
            vm((3, NZ, 8, 512), F32),
            vm((NZ - 1, 8, 512), F32), vm((8, HALF), BF16), vm((8, HALF), F32), vm((8, HALF), F32),
            vm((4, SM, SM), F32), vm((4, SM, SM), F32),
            dma((2,)), dma, dma, dma((3,)), dma((3,)), dma((6,)), dma((6,)), dma((3,)), dma((3,)),
            dma((7,)), dma((7,)), dma, dma, dma, dma,
            dma((7,)), dma((7,)), dma((5, 4)), dma((5, 4)), dma((16,)), dma((16,)), dma((3,)),
        ],
        compiler_params=pltpu.CompilerParams(collective_id=1, has_side_effects=True),
        name="routed",
    )(embeddings, dest, slot, centroids, rank)


BLOCKS = (4, 5, 6, 11, 0, 1, 12, 13, 2, 3, 7, 8, 9, 10)


def permuted(lo_map, hi_map, hot_ref, lo_ref, hi_ref, gram_ref, out_ref, moment_ref):
    del lo_map, hi_map

    @pl.when(pl.program_id(0) < 4)
    def _():
        moment_ref[...] = gram_ref[...]

    both = jnp.concatenate([lo_ref[...], hi_ref[...]], axis=1)
    out_ref[...] = jnp.dot(hot_ref[...], both, preferred_element_type=F32).astype(BF16)


def permute(table, hot, gram):
    k = table.shape[0]
    return pl.pallas_call(
        permuted,
        grid_spec=pltpu.PrefetchScalarGridSpec(
            num_scalar_prefetch=2,
            grid=(7,),
            in_specs=[
                pl.BlockSpec((k, k), lambda j, lo, hi: (0, 0)),
                pl.BlockSpec((k, 128), lambda j, lo, hi: (0, lo[j])),
                pl.BlockSpec((k, 128), lambda j, lo, hi: (0, hi[j])),
                pl.BlockSpec((1, SM, SM), lambda j, lo, hi: (jnp.minimum(j, 3), 0, 0)),
            ],
            out_specs=(
                pl.BlockSpec((k, 256), lambda j, lo, hi: (0, j)),
                pl.BlockSpec((1, SM, SM), lambda j, lo, hi: (jnp.minimum(j, 3), 0, 0)),
            ),
        ),
        out_shape=(jax.ShapeDtypeStruct((k, WIDE), BF16), jax.ShapeDtypeStruct(gram.shape, F32)),
        name="permuted",
    )(jnp.array(BLOCKS[0::2], jnp.int32), jnp.array(BLOCKS[1::2], jnp.int32), hot, table, table, gram)


def on_device(embeddings, owner_dest, cluster_slot, cluster_rank, centroids):
    n = embeddings.shape[0]
    k = cluster_rank.shape[0]
    table, gram, hot = route(embeddings, owner_dest.reshape(1, n), cluster_slot.reshape(1, n), centroids,
                             cluster_rank.reshape(1, k))
    return permute(table.reshape(k, WIDE), hot, gram)


def solution(mesh):
    placed = (
        P(("dp", "grp"), None),
        P(("dp", "grp"), None),
        P(("dp", "grp"), None),
        P(),
        P("dp", None),
    )
    return jax.shard_map(
        on_device,
        mesh=mesh,
        in_specs=placed,
        out_specs=(P(), P(("dp", "grp"), None, None)),
        check_vma=False,
    )
```

```python
import functools

import jax
import jax.numpy as jnp
from jax import lax
from jax.experimental import pallas as pl
from jax.experimental.pallas import tpu as pltpu
from jax.sharding import PartitionSpec as P

WIDE = 1792
HALF = 896
NX, NY, NZ = 4, 4, 8
CHIPS = 128
SM = 256
MESH = pl.DeviceIdType.MESH
F32 = jnp.float32
BF16 = jnp.bfloat16
EPS = 1e-06


def iota(shape, dim):
    return lax.broadcasted_iota(jnp.int32, shape, dim)


def thirds(v):
    hi = v.astype(BF16)
    rest = v - hi.astype(F32)
    mid = rest.astype(BF16)
    return hi, mid, (rest - mid.astype(F32)).astype(BF16)


def row_of(col):
    n = col.shape[0]
    eye = iota((n, n), 0) == iota((n, n), 1)
    return jnp.sum(jnp.where(eye, col, 0.0), axis=0, keepdims=True)


def col_of(row):
    n = row.shape[1]
    eye = iota((n, n), 0) == iota((n, n), 1)
    return jnp.sum(jnp.where(eye, row, 0.0), axis=1, keepdims=True)


def scales(rows):
    sq = rows * rows
    s512 = jnp.sum(sq[:, :512], axis=1, keepdims=True)
    s1024 = s512 + jnp.sum(sq[:, 512:], axis=1, keepdims=True)
    return lax.rsqrt(s512 * (1.0 / 512) + EPS), lax.rsqrt(s1024 * (1.0 / 1024) + EPS)


def bits(mask):
    return mask.astype(F32).astype(BF16)


def pack(emb_ref, dest, slot, r512, r1024, sendbuf):
    n = dest.shape[1]
    hits = iota((CHIPS, n), 0) == dest
    owner = bits(hits)
    earlier = bits(iota((n, n), 0) < iota((n, n), 1))
    before = jnp.dot(owner, earlier, preferred_element_type=F32)
    pos = jnp.sum(jnp.where(hits, before, 0.0), axis=0, keepdims=True).astype(jnp.int32)
    values = [slot.astype(F32) + 1.0]
    for s in (r512, r1024):
        values += [t.astype(F32) for t in thirds(s)]
    line = iota((128, n), 0)
    tags = jnp.zeros((128, n), F32)
    for i, v in enumerate(values):
        tags = jnp.where((line & 15) == i, v, tags)
    tags = jnp.where((line >> 4) == pos, tags, 0.0).astype(BF16)
    tags = lax.dot_general(owner, tags, (((1,), (1,)), ((), ())), preferred_element_type=F32)
    place = bits(iota((CHIPS * 8, n), 0) == dest * 8 + pos)
    rows = jnp.dot(place, emb_ref[:, :SM], preferred_element_type=F32).reshape(CHIPS, 8, SM)
    wide = jnp.concatenate([tags, jnp.zeros((CHIPS, SM - 128), F32)], axis=1)
    rows = jnp.where(iota((CHIPS, 8, SM), 1) == 6, wide[:, None, :], rows)
    sendbuf[...] = rows.astype(BF16)


def order_of(dest, slot, g):
    xx, zz, yy = dest & 3, (dest >> 2) & 7, dest >> 5
    a = xx * (1 - g) + yy * g
    b = yy * (1 - g) + xx * g
    return ((a * 4 + b) * 8 + zz) * 8 + slot


def columns(g):
    return (pl.ds(pl.multiple_of(256 + g * 256, 256), 256), pl.ds(pl.multiple_of(256 + g * 512, 256), 256))


def whole(order, xs, ss, total, add):
    k = 8 * CHIPS
    hot = bits(iota((k, order.shape[1]), 0) == order)
    hot = jnp.concatenate([hot, hot, hot], axis=1)
    for at, x, s in zip((0, 256), xs, ss):
        acc = jnp.dot(hot, jnp.concatenate(thirds(x.astype(F32) * s), axis=0), preferred_element_type=F32)
        acc = acc.reshape(4, 4, NZ, 8, 256)
        if add:
            acc = acc + total[:, :, :, :, at:at + 256]
        total[:, :, :, :, at:at + 256] = acc


def routed(emb_ref, dest_ref, slot_ref, cent_ref, rank_ref, table_out, gram_out, hot_out, table_ref, gram_ref, hot_ref,
           sendbuf, recvbuf, pxa, pxb, info, pinfo, total, half1, full1, full2, zgot, blk, psums, osums,
           pgram, ogram,
           own_sem, a2s, a2r, xs, xr, r1s, r1r, r2s, r2r, z3s, z3r, pss, psr, pgs, pgr,
           zs, zr, as_, ar, ps, pr, outs):
    dp = lax.axis_index("dp")
    g = lax.axis_index("grp")
    x = dp % NX
    z = (dp // NX) % NZ
    y = dp // (NX * NZ)
    h = 1 - g
    partner = (dp, h)
    barrier = pltpu.get_barrier_semaphore()
    pl.semaphore_signal(barrier, inc=1, device_id=partner, device_id_type=MESH)

    xs4 = [(x + 2 + k) % NX for k in range(4)]

    def others(body):
        def along(first, last, base, ks):
            def step(j, c):
                at = (base + (z + 4 + j) % NZ) * NX
                for k in ks:
                    body(at + xs4[k])
                return c
            lax.fori_loop(first, last, step, 0)

        for i in range(NY):
            base = ((y + 2 + i) % NY) * NZ
            if i == 2:
                along(0, NZ, base, (0, 1, 3))
                along(0, 4, base, (2,))
                along(5, NZ, base, (2,))
            else:
                along(0, NZ, base, range(4))

    def greet(t):
        pl.semaphore_signal(barrier, inc=1, device_id=(t, g), device_id_type=MESH)

    others(greet)
    dest, slot = dest_ref[...], slot_ref[...]
    c512, c1024 = scales(emb_ref[...].astype(F32))
    r512, r1024 = row_of(c512), row_of(c1024)
    gf = g.astype(F32)
    info[...] = jnp.zeros_like(info)
    info[0:1, :] = order_of(dest, slot, h).astype(F32)
    info[1:2, :] = r512 * gf + r1024 * (1.0 - gf)
    info[2:3, :] = r1024
    ca, cb = columns(g)
    whole(order_of(dest, slot, g), (emb_ref[:, ca], emb_ref[:, cb]), (c512 * (1.0 - gf) + c1024 * gf, c1024), total, False)
    pl.semaphore_wait(barrier, CHIPS)

    sent = []

    def send(src, dst, ss, rs, peer):
        c = pltpu.make_async_remote_copy(src_ref=src, dst_ref=dst, send_sem=ss, recv_sem=rs,
                                         device_id=peer, device_id_type=MESH)
        c.start()
        sent.append(c)

    def got(ref, sem):
        pltpu.make_async_copy(ref, ref, sem).wait()

    pa, pb = columns(h)
    send(info, pinfo, xs.at[0], xr.at[0], partner)
    send(emb_ref.at[:, pa], pxa, xs.at[1], xr.at[1], partner)
    send(emb_ref.at[:, pb], pxb, xs.at[2], xr.at[2], partner)
    pack(emb_ref, dest, slot, r512, r1024, sendbuf)
    mine = pltpu.make_async_copy(sendbuf.at[dp], recvbuf.at[dp], own_sem.at[0])
    mine.start()
    got(pinfo, xr.at[0])
    got(pxa, xr.at[1])
    got(pxb, xr.at[2])
    whole(pinfo[0:1, :].astype(jnp.int32), (pxa[...], pxb[...]), (col_of(pinfo[1:2, :]), col_of(pinfo[2:3, :])), total, True)

    def scatter(t):
        pltpu.make_async_remote_copy(src_ref=sendbuf.at[t], dst_ref=recvbuf.at[dp], send_sem=a2s, recv_sem=a2r,
                                     device_id=(t, g), device_id_type=MESH).start()

    def to(i, j):
        yy, xx = (y + 4 + i * g + j * h) % NY, (x + 4 + i * h + j * g) % NX
        return ((yy * NZ + z) * NX + xx, g)

    p = x * h + y * g
    q = y * h + x * g

    def ring(at, me, lo, hi, half, full, plus, minus, ss, rs, between):
        up, down, far = (me + 1) % 4, (me + 3) % 4, (me + 2) % 4
        send(at(far, lo), half.at[0], ss.at[0], rs.at[0], plus)
        send(at(far, hi), half.at[1], ss.at[1], rs.at[1], minus)
        send(at(up, hi), full.at[0, hi], ss.at[2], rs.at[2], plus)
        send(at(down, lo), full.at[1, lo], ss.at[3], rs.at[3], minus)
        got(half.at[0], rs.at[0])
        ref = at(up, lo)
        ref[...] = ref[...] + half[0]
        send(ref, full.at[0, lo], ss.at[4], rs.at[4], plus)
        got(half.at[1], rs.at[1])
        ref = at(down, hi)
        ref[...] = ref[...] + half[1]
        send(ref, full.at[1, hi], ss.at[5], rs.at[5], minus)
        between()
        got(full.at[0, hi], rs.at[2])
        got(full.at[1, lo], rs.at[3])
        got(full.at[0, lo], rs.at[4])
        got(full.at[1, hi], rs.at[5])
        for part in (lo, hi):
            ref = at(me, part)
            ref[...] = ref[...] + full[0, part] + full[1, part]

    ring(lambda i, s: total.at[i, s], p, pl.ds(0, 2), pl.ds(2, 2), half1, full1, to(1, 0), to(-1, 0), r1s, r1r,
         lambda: others(scatter))
    for i in (2, 1, 3):
        send(total.at[p, (q + i) % 4], full2.at[i - 1], r2s.at[i - 1], r2r.at[i - 1], to(0, i))
    for i in (1, 3, 2):
        got(full2.at[i - 1], r2r.at[i - 1])
    total[p, q] = total[p, q] + full2[0] + full2[1] + full2[2]

    def along_z(d):
        return ((y * NZ + (z + d) % NZ) * NX + x, g)

    for d in range(1, NZ):
        send(total.at[p, q, (z + d) % NZ], zgot.at[d - 1], z3s.at[d - 1], z3r.at[d - 1], along_z(d))

    mine.wait()
    every = recvbuf.at[pl.ds(0, CHIPS - 1)]
    got(every, a2r)
    rows = recvbuf[...].astype(F32)
    slots = CHIPS * 8
    tags = jnp.broadcast_to(rows[:, 6:7, :128], (CHIPS, 8, 128)).reshape(slots, 128)
    lane = iota((slots, 128), 1)
    tags = jnp.where((lane >> 4) == (iota((slots, 128), 0) & 7), tags, 0.0).astype(BF16)
    f = iota((128, 128), 0) & 15
    c = iota((128, 128), 1)
    pick = ((f == 0) & (c == 0)) | ((f >= 1) & (f <= 3) & (c == 1)) | ((f >= 4) & (f <= 6) & (c == 2))
    vals = jnp.dot(tags, pick.astype(F32).astype(BF16), preferred_element_type=F32)
    idrow = vals.T[0:1, :]
    selt = (idrow == (iota((8, slots), 0) + 1).astype(F32)).astype(F32)
    sel = (vals[:, 0:1] == (iota((slots, 8), 1) + 1).astype(F32)).astype(F32).astype(BF16)
    cent = jnp.dot(sel, cent_ref[:, :SM], preferred_element_type=F32)
    rows = rows.reshape(slots, SM)
    s256 = lax.rsqrt(jnp.sum(rows * rows, axis=1, keepdims=True) * (1.0 / 256) + EPS)
    small = (rows * s256 - cent).astype(BF16)
    seltb = selt.astype(BF16)
    osums[:, 0:256] = jnp.dot(seltb, small, preferred_element_type=F32)
    osums[:, 256:512] = jnp.dot(seltb, (rows * vals[:, 1:2] - cent).astype(BF16), preferred_element_type=F32)
    osums[:, 512:768] = jnp.dot(seltb, (rows * vals[:, 2:3] - cent).astype(BF16), preferred_element_type=F32)
    osums[:, 768:896] = jnp.broadcast_to(jnp.sum(selt, axis=1, keepdims=True), (8, 128))
    send(osums, psums, pss, psr, partner)
    smallt = small.astype(F32).T

    def gram(c):
        keep = idrow == (c + 1).astype(F32)
        return jnp.dot(jnp.where(keep, smallt, 0.0).astype(BF16), small, preferred_element_type=F32)

    for d in range(1, NZ):
        got(zgot.at[d - 1], z3r.at[d - 1])
    got(psums, psr)
    sums = osums[...] + psums[...]
    count = sums[:, 768:769]
    denom = count + 1.0
    big = total[p, q, z]
    for d in range(1, NZ):
        big = big + zgot[d - 1]
    blk[:, 0:256] = ((big[:, :256] - count * cent_ref[:, ca].astype(F32)) / denom).astype(BF16)
    blk[:, 256:512] = ((big[:, 256:] - count * cent_ref[:, cb].astype(F32)) / denom).astype(BF16)
    part = jnp.where(gf > 0.5, sums[:, 384:768], sums[:, 0:384])
    blk[:, 512:896] = (part / denom).astype(BF16)

    cols = pl.ds(pl.multiple_of(g * HALF, 128), HALF)
    pcols = pl.ds(pl.multiple_of(h * HALF, 128), HALF)

    def chunk(i, j, z0=0, nz=NZ, at=cols):
        yy, xx = (y + 4 + i * g + j * h) % NY, (x + 4 + i * h + j * g) % NX
        return table_ref.at[yy, pl.ds(z0, nz), xx, :, at]

    home = table_ref.at[y, z, x, :, cols]
    for d in range(1, NZ):
        send(blk, home, zs.at[d - 1], zr.at[d - 1], along_z(d))
    own = pltpu.make_async_copy(blk, home, own_sem.at[1])
    own.start()
    for c in range(4):
        pgram[c] = gram(h * 4 + c)
    send(pgram, ogram, pgs, pgr, partner)
    for b in range(8):
        piece = rank_ref[:, b * 128:(b + 1) * 128].astype(F32)
        col = col_of(piece).astype(jnp.int32)
        hot_ref[b * 128:(b + 1) * 128, :] = bits(iota((128, 1024), 1) == col)
    hot_copy = pltpu.make_async_copy(hot_ref, hot_out, outs.at[0])
    hot_copy.start()
    own.wait()
    for d in range(1, NZ):
        got(home, zr.at[d - 1])

    seen = []

    def keep(yy, xx, at):
        pltpu.make_async_copy(table_ref.at[yy, :, xx, :, at], table_out.at[yy, :, xx, :, at], outs.at[1]).start()

    def take(k):
        i, j = seen[k]
        yy, xx = (y + 4 + i * h + j * g) % NY, (x + 4 + i * g + j * h) % NX
        got(table_ref.at[yy, :, xx, :, pcols], pr.at[k])
        keep(yy, xx, pcols)

    def share(i, j):
        k = len(seen)
        seen.append((i, j))
        send(chunk(i, j), chunk(i, j), ps.at[k], pr.at[k], partner)
        keep((y + 4 + i * g + j * h) % NY, (x + 4 + i * h + j * g) % NX, cols)
        if k >= 5:
            take(k - 5)

    def out(row, here, along, far):
        send(here, here, as_.at[row, 0], ar.at[row, 0], along(1))
        send(here, here, as_.at[row, 1], ar.at[row, 1], along(-1))
        if far:
            send(here, here, as_.at[row, 2], ar.at[row, 2], along(2))

    def first(i):
        return to(i, 0)

    def second(i):
        return to(0, i)

    out(0, chunk(0, 0), first, True)
    out(1, chunk(0, 0), second, False)
    share(0, 0)
    for c in range(4):
        gram_ref[c] = gram(g * 4 + c)
    got(chunk(-1, 0), ar.at[0, 0])
    out(2, chunk(-1, 0), second, False)
    got(chunk(1, 0), ar.at[0, 1])
    out(3, chunk(1, 0), second, False)
    share(-1, 0)
    share(1, 0)

    def pass_on(row, i):
        got(chunk(i, -1), ar.at[row, 0])
        lo = chunk(i, -1, 0, 4)
        send(lo, lo, as_.at[row, 2], ar.at[row, 2], to(0, 1))
        got(chunk(i, 1), ar.at[row, 1])
        hi = chunk(i, 1, 4, 4)
        send(hi, hi, as_.at[row, 3], ar.at[row, 3], to(0, -1))
        share(i, -1)
        share(i, 1)

    pass_on(1, 0)
    got(chunk(2, 0), ar.at[0, 2])
    out(4, chunk(2, 0), second, True)
    share(2, 0)
    pass_on(2, -1)
    pass_on(3, 1)
    got(ogram, pgr)
    for c in range(4):
        one = jnp.sum(jnp.where(iota((8, 1), 0) == g * 4 + c, denom, 0.0), axis=0, keepdims=True)
        gram_ref[c] = (gram_ref[c] + ogram[c]) / one
    gram_copy = pltpu.make_async_copy(gram_ref, gram_out, outs.at[2])
    gram_copy.start()
    for row, i in ((1, 0), (2, -1), (3, 1)):
        got(chunk(i, 2, 0, 4), ar.at[row, 2])
        got(chunk(i, 2, 4, 4), ar.at[row, 3])
        share(i, 2)
    for n, i in enumerate((-1, 1, 2)):
        got(chunk(2, i), ar.at[4, n])
        share(2, i)
    for k in range(11, 16):
        take(k)
    hot_copy.wait()
    gram_copy.wait()
    pltpu.make_async_copy(table_ref, table_out, outs.at[1]).wait()
    got(sendbuf.at[pl.ds(0, CHIPS - 1)], a2s)
    for c in sent:
        c.wait_send()


def route(embeddings, dest, slot, centroids, rank):
    dma = pltpu.SemaphoreType.DMA
    vm = pltpu.VMEM
    n = embeddings.shape[0]
    here = pl.BlockSpec(memory_space=pltpu.VMEM)
    return pl.pallas_call(
        routed,
        out_shape=(jax.ShapeDtypeStruct((NY, NZ, NX, 8, WIDE), BF16), jax.ShapeDtypeStruct((4, SM, SM), F32),
                   jax.ShapeDtypeStruct((1024, 1024), BF16)),
        in_specs=[here] * 5,
        out_specs=(pl.BlockSpec(memory_space=pl.ANY),) * 3,
        scratch_shapes=[
            vm((NY, NZ, NX, 8, WIDE), BF16), vm((4, SM, SM), F32), vm((1024, 1024), BF16),
            vm((CHIPS, 8, SM), BF16), vm((CHIPS, 8, SM), BF16),
            vm((n, 256), BF16), vm((n, 256), BF16), vm((8, n), F32), vm((8, n), F32),
            vm((4, 4, NZ, 8, 512), F32),
            vm((2, 2, NZ, 8, 512), F32), vm((2, 4, NZ, 8, 512), F32),
            vm((3, NZ, 8, 512), F32),
            vm((NZ - 1, 8, 512), F32), vm((8, HALF), BF16), vm((8, HALF), F32), vm((8, HALF), F32),
            vm((4, SM, SM), F32), vm((4, SM, SM), F32),
            dma((2,)), dma, dma, dma((3,)), dma((3,)), dma((6,)), dma((6,)), dma((3,)), dma((3,)),
            dma((7,)), dma((7,)), dma, dma, dma, dma,
            dma((7,)), dma((7,)), dma((5, 4)), dma((5, 4)), dma((16,)), dma((16,)), dma((3,)),
        ],
        compiler_params=pltpu.CompilerParams(collective_id=1, has_side_effects=True),
        name="routed",
    )(embeddings, dest, slot, centroids, rank)


PARTS = (
    (0, ((512, 896), (1408, 1536))),
    (512, ((0, 256),)),
    (768, ((1536, 1792),)),
    (1024, ((256, 512),)),
    (1280, ((896, 1408),)),
)


def permuted(hot_ref, table_ref, gram_ref, out_ref, moment_ref):
    moment_ref[...] = gram_ref[...]
    hot = hot_ref[...]
    for at, spans in PARTS:
        cols = [table_ref[:, lo:hi] for lo, hi in spans]
        cols = cols[0] if len(cols) == 1 else jnp.concatenate(cols, axis=1)
        out_ref[:, at:at + cols.shape[1]] = jnp.dot(hot, cols, preferred_element_type=F32).astype(BF16)


def permute(table, hot, gram):
    k = table.shape[0]
    one = pl.BlockSpec((1, SM, SM), lambda j: (j, 0, 0))
    return pl.pallas_call(
        permuted,
        grid=(4,),
        in_specs=[
            pl.BlockSpec((k // 4, k), lambda j: (j, 0)),
            pl.BlockSpec((k, WIDE), lambda j: (0, 0)),
            one,
        ],
        out_specs=(pl.BlockSpec((k // 4, WIDE), lambda j: (j, 0)), one),
        out_shape=(jax.ShapeDtypeStruct((k, WIDE), BF16), jax.ShapeDtypeStruct(gram.shape, F32)),
        name="permuted",
    )(hot, table, gram)


def on_device(embeddings, owner_dest, cluster_slot, cluster_rank, centroids):
    n = embeddings.shape[0]
    k = cluster_rank.shape[0]
    table, gram, hot = route(embeddings, owner_dest.reshape(1, n), cluster_slot.reshape(1, n), centroids,
                             cluster_rank.reshape(1, k))
    return permute(table.reshape(k, WIDE), hot, gram)


def solution(mesh):
    placed = (
        P(("dp", "grp"), None),
        P(("dp", "grp"), None),
        P(("dp", "grp"), None),
        P(),
        P("dp", None),
    )
    return jax.shard_map(
        on_device,
        mesh=mesh,
        in_specs=placed,
        out_specs=(P(), P(("dp", "grp"), None, None)),
        check_vma=False,
    )
```

```python
import functools

import jax
import jax.numpy as jnp
from jax import lax
from jax.experimental import pallas as pl
from jax.experimental.pallas import tpu as pltpu
from jax.sharding import PartitionSpec as P

WIDE = 1792
HALF = 896
NX, NY, NZ = 4, 4, 8
CHIPS = 128
SM = 256
MESH = pl.DeviceIdType.MESH
F32 = jnp.float32
BF16 = jnp.bfloat16
EPS = 1e-06


def iota(shape, dim):
    return lax.broadcasted_iota(jnp.int32, shape, dim)


def thirds(v):
    hi = v.astype(BF16)
    rest = v - hi.astype(F32)
    mid = rest.astype(BF16)
    return hi, mid, (rest - mid.astype(F32)).astype(BF16)


def row_of(col):
    n = col.shape[0]
    eye = iota((n, n), 0) == iota((n, n), 1)
    return jnp.sum(jnp.where(eye, col, 0.0), axis=0, keepdims=True)


def col_of(row):
    n = row.shape[1]
    eye = iota((n, n), 0) == iota((n, n), 1)
    return jnp.sum(jnp.where(eye, row, 0.0), axis=1, keepdims=True)


def scales(rows):
    sq = rows * rows
    s512 = jnp.sum(sq[:, :512], axis=1, keepdims=True)
    s1024 = s512 + jnp.sum(sq[:, 512:], axis=1, keepdims=True)
    return lax.rsqrt(s512 * (1.0 / 512) + EPS), lax.rsqrt(s1024 * (1.0 / 1024) + EPS)


def bits(mask):
    return mask.astype(F32).astype(BF16)


def pack(emb_ref, dest, slot, r512, r1024, sendbuf):
    n = dest.shape[1]
    hits = iota((CHIPS, n), 0) == dest
    owner = bits(hits)
    earlier = bits(iota((n, n), 0) < iota((n, n), 1))
    before = jnp.dot(owner, earlier, preferred_element_type=F32)
    pos = jnp.sum(jnp.where(hits, before, 0.0), axis=0, keepdims=True).astype(jnp.int32)
    values = [slot.astype(F32) + 1.0]
    for s in (r512, r1024):
        values += [t.astype(F32) for t in thirds(s)]
    line = iota((128, n), 0)
    tags = jnp.zeros((128, n), F32)
    for i, v in enumerate(values):
        tags = jnp.where((line & 15) == i, v, tags)
    tags = jnp.where((line >> 4) == pos, tags, 0.0).astype(BF16)
    tags = lax.dot_general(owner, tags, (((1,), (1,)), ((), ())), preferred_element_type=F32)
    place = bits(iota((CHIPS * 8, n), 0) == dest * 8 + pos)
    rows = jnp.dot(place, emb_ref[:, :SM], preferred_element_type=F32).reshape(CHIPS, 8, SM)
    wide = jnp.concatenate([tags, jnp.zeros((CHIPS, SM - 128), F32)], axis=1)
    rows = jnp.where(iota((CHIPS, 8, SM), 1) == 6, wide[:, None, :], rows)
    sendbuf[...] = rows.astype(BF16)


def order_of(dest, slot, g):
    xx, zz, yy = dest & 3, (dest >> 2) & 7, dest >> 5
    a = xx * (1 - g) + yy * g
    b = yy * (1 - g) + xx * g
    return ((a * 4 + b) * 8 + zz) * 8 + slot


def columns(g):
    return (pl.ds(pl.multiple_of(256 + g * 256, 256), 256), pl.ds(pl.multiple_of(256 + g * 512, 256), 256))


def whole(order, xs, ss, total, add):
    k = 8 * CHIPS
    hot = bits(iota((k, order.shape[1]), 0) == order)
    hot = jnp.concatenate([hot, hot, hot], axis=1)
    for at, x, s in zip((0, 256), xs, ss):
        acc = jnp.dot(hot, jnp.concatenate(thirds(x.astype(F32) * s), axis=0), preferred_element_type=F32)
        acc = acc.reshape(4, 4, NZ, 8, 256)
        if add:
            acc = acc + total[:, :, :, :, at:at + 256]
        total[:, :, :, :, at:at + 256] = acc


def routed(emb_in, dest_in, slot_in, cent_in, rank_in, table_ref, gram_out, hot_out,
           emb_ref, dest_ref, slot_ref, cent_ref, rank_ref, gram_ref, hot_ref,
           sendbuf, recvbuf, pxa, pxb, info, pinfo, total, half1, full1, full2, zgot, blk, psums, osums,
           pgram, ogram,
           own_sem, a2s, a2r, xs, xr, r1s, r1r, r2s, r2r, z3s, z3r, pss, psr, pgs, pgr,
           zs, zr, as_, ar, ps, pr, outs, ins):
    dp = lax.axis_index("dp")
    g = lax.axis_index("grp")
    x = dp % NX
    z = (dp // NX) % NZ
    y = dp // (NX * NZ)
    h = 1 - g
    partner = (dp, h)
    loads = [pltpu.make_async_copy(src, dst, ins.at[i]) for i, (src, dst) in enumerate(
        ((emb_in, emb_ref), (dest_in, dest_ref), (slot_in, slot_ref), (cent_in, cent_ref), (rank_in, rank_ref)))]
    for c in loads:
        c.start()
    barrier = pltpu.get_barrier_semaphore()
    pl.semaphore_signal(barrier, inc=1, device_id=partner, device_id_type=MESH)

    xs4 = [(x + 2 + k) % NX for k in range(4)]

    def others(body):
        def along(first, last, base, ks):
            def step(j, c):
                at = (base + (z + 4 + j) % NZ) * NX
                for k in ks:
                    body(at + xs4[k])
                return c
            lax.fori_loop(first, last, step, 0)

        for i in range(NY):
            base = ((y + 2 + i) % NY) * NZ
            if i == 2:
                along(0, NZ, base, (0, 1, 3))
                along(0, 4, base, (2,))
                along(5, NZ, base, (2,))
            else:
                along(0, NZ, base, range(4))

    def greet(t):
        pl.semaphore_signal(barrier, inc=1, device_id=(t, g), device_id_type=MESH)

    others(greet)
    for c in loads:
        c.wait()
    dest, slot = dest_ref[...], slot_ref[...]
    c512, c1024 = scales(emb_ref[...].astype(F32))
    r512, r1024 = row_of(c512), row_of(c1024)
    gf = g.astype(F32)
    info[...] = jnp.zeros_like(info)
    info[0:1, :] = order_of(dest, slot, h).astype(F32)
    info[1:2, :] = r512 * gf + r1024 * (1.0 - gf)
    info[2:3, :] = r1024
    ca, cb = columns(g)
    whole(order_of(dest, slot, g), (emb_ref[:, ca], emb_ref[:, cb]), (c512 * (1.0 - gf) + c1024 * gf, c1024), total, False)
    pl.semaphore_wait(barrier, CHIPS)

    sent = []

    def send(src, dst, ss, rs, peer):
        c = pltpu.make_async_remote_copy(src_ref=src, dst_ref=dst, send_sem=ss, recv_sem=rs,
                                         device_id=peer, device_id_type=MESH)
        c.start()
        sent.append(c)

    def got(ref, sem):
        pltpu.make_async_copy(ref, ref, sem).wait()

    pa, pb = columns(h)
    send(info, pinfo, xs.at[0], xr.at[0], partner)
    send(emb_ref.at[:, pa], pxa, xs.at[1], xr.at[1], partner)
    send(emb_ref.at[:, pb], pxb, xs.at[2], xr.at[2], partner)
    pack(emb_ref, dest, slot, r512, r1024, sendbuf)
    mine = pltpu.make_async_copy(sendbuf.at[dp], recvbuf.at[dp], own_sem.at[0])
    mine.start()
    got(pinfo, xr.at[0])
    got(pxa, xr.at[1])
    got(pxb, xr.at[2])
    whole(pinfo[0:1, :].astype(jnp.int32), (pxa[...], pxb[...]), (col_of(pinfo[1:2, :]), col_of(pinfo[2:3, :])), total, True)

    def scatter(t):
        pltpu.make_async_remote_copy(src_ref=sendbuf.at[t], dst_ref=recvbuf.at[dp], send_sem=a2s, recv_sem=a2r,
                                     device_id=(t, g), device_id_type=MESH).start()

    def to(i, j):
        yy, xx = (y + 4 + i * g + j * h) % NY, (x + 4 + i * h + j * g) % NX
        return ((yy * NZ + z) * NX + xx, g)

    p = x * h + y * g
    q = y * h + x * g

    def ring(at, me, lo, hi, half, full, plus, minus, ss, rs, between):
        up, down, far = (me + 1) % 4, (me + 3) % 4, (me + 2) % 4
        send(at(far, lo), half.at[0], ss.at[0], rs.at[0], plus)
        send(at(far, hi), half.at[1], ss.at[1], rs.at[1], minus)
        send(at(up, hi), full.at[0, hi], ss.at[2], rs.at[2], plus)
        send(at(down, lo), full.at[1, lo], ss.at[3], rs.at[3], minus)
        got(half.at[0], rs.at[0])
        ref = at(up, lo)
        ref[...] = ref[...] + half[0]
        send(ref, full.at[0, lo], ss.at[4], rs.at[4], plus)
        got(half.at[1], rs.at[1])
        ref = at(down, hi)
        ref[...] = ref[...] + half[1]
        send(ref, full.at[1, hi], ss.at[5], rs.at[5], minus)
        between()
        got(full.at[0, hi], rs.at[2])
        got(full.at[1, lo], rs.at[3])
        got(full.at[0, lo], rs.at[4])
        got(full.at[1, hi], rs.at[5])
        for part in (lo, hi):
            ref = at(me, part)
            ref[...] = ref[...] + full[0, part] + full[1, part]

    ring(lambda i, s: total.at[i, s], p, pl.ds(0, 2), pl.ds(2, 2), half1, full1, to(1, 0), to(-1, 0), r1s, r1r,
         lambda: others(scatter))
    for i in (2, 1, 3):
        send(total.at[p, (q + i) % 4], full2.at[i - 1], r2s.at[i - 1], r2r.at[i - 1], to(0, i))
    for i in (1, 3, 2):
        got(full2.at[i - 1], r2r.at[i - 1])
    total[p, q] = total[p, q] + full2[0] + full2[1] + full2[2]

    def along_z(d):
        return ((y * NZ + (z + d) % NZ) * NX + x, g)

    for d in range(1, NZ):
        send(total.at[p, q, (z + d) % NZ], zgot.at[d - 1], z3s.at[d - 1], z3r.at[d - 1], along_z(d))

    mine.wait()
    every = recvbuf.at[pl.ds(0, CHIPS - 1)]
    got(every, a2r)
    rows = recvbuf[...].astype(F32)
    slots = CHIPS * 8
    tags = jnp.broadcast_to(rows[:, 6:7, :128], (CHIPS, 8, 128)).reshape(slots, 128)
    lane = iota((slots, 128), 1)
    tags = jnp.where((lane >> 4) == (iota((slots, 128), 0) & 7), tags, 0.0).astype(BF16)
    f = iota((128, 128), 0) & 15
    c = iota((128, 128), 1)
    pick = ((f == 0) & (c == 0)) | ((f >= 1) & (f <= 3) & (c == 1)) | ((f >= 4) & (f <= 6) & (c == 2))
    vals = jnp.dot(tags, pick.astype(F32).astype(BF16), preferred_element_type=F32)
    idrow = vals.T[0:1, :]
    selt = (idrow == (iota((8, slots), 0) + 1).astype(F32)).astype(F32)
    sel = (vals[:, 0:1] == (iota((slots, 8), 1) + 1).astype(F32)).astype(F32).astype(BF16)
    cent = jnp.dot(sel, cent_ref[:, :SM], preferred_element_type=F32)
    rows = rows.reshape(slots, SM)
    s256 = lax.rsqrt(jnp.sum(rows * rows, axis=1, keepdims=True) * (1.0 / 256) + EPS)
    small = (rows * s256 - cent).astype(BF16)
    seltb = selt.astype(BF16)
    osums[:, 0:256] = jnp.dot(seltb, small, preferred_element_type=F32)
    osums[:, 256:512] = jnp.dot(seltb, (rows * vals[:, 1:2] - cent).astype(BF16), preferred_element_type=F32)
    osums[:, 512:768] = jnp.dot(seltb, (rows * vals[:, 2:3] - cent).astype(BF16), preferred_element_type=F32)
    osums[:, 768:896] = jnp.broadcast_to(jnp.sum(selt, axis=1, keepdims=True), (8, 128))
    send(osums, psums, pss, psr, partner)
    smallt = small.astype(F32).T

    def gram(c):
        keep = idrow == (c + 1).astype(F32)
        return jnp.dot(jnp.where(keep, smallt, 0.0).astype(BF16), small, preferred_element_type=F32)

    for d in range(1, NZ):
        got(zgot.at[d - 1], z3r.at[d - 1])
    got(psums, psr)
    sums = osums[...] + psums[...]
    count = sums[:, 768:769]
    denom = count + 1.0
    big = total[p, q, z]
    for d in range(1, NZ):
        big = big + zgot[d - 1]
    blk[:, 0:256] = ((big[:, :256] - count * cent_ref[:, ca].astype(F32)) / denom).astype(BF16)
    blk[:, 256:512] = ((big[:, 256:] - count * cent_ref[:, cb].astype(F32)) / denom).astype(BF16)
    part = jnp.where(gf > 0.5, sums[:, 384:768], sums[:, 0:384])
    blk[:, 512:896] = (part / denom).astype(BF16)

    cols = pl.ds(pl.multiple_of(g * HALF, 128), HALF)
    pcols = pl.ds(pl.multiple_of(h * HALF, 128), HALF)

    def chunk(i, j, z0=0, nz=NZ, at=cols):
        yy, xx = (y + 4 + i * g + j * h) % NY, (x + 4 + i * h + j * g) % NX
        return table_ref.at[yy, pl.ds(z0, nz), xx, :, at]

    home = table_ref.at[y, z, x, :, cols]
    for d in range(1, NZ):
        send(blk, home, zs.at[d - 1], zr.at[d - 1], along_z(d))
    own = pltpu.make_async_copy(blk, home, own_sem.at[1])
    own.start()
    for c in range(4):
        pgram[c] = gram(h * 4 + c)
    send(pgram, ogram, pgs, pgr, partner)
    for b in range(8):
        piece = rank_ref[:, b * 128:(b + 1) * 128].astype(F32)
        col = col_of(piece).astype(jnp.int32)
        hot_ref[b * 128:(b + 1) * 128, :] = bits(iota((128, 1024), 1) == col)
    hot_copy = pltpu.make_async_copy(hot_ref, hot_out, outs.at[0])
    hot_copy.start()
    own.wait()
    for d in range(1, NZ):
        got(home, zr.at[d - 1])

    seen = []

    def take(k):
        i, j = seen[k]
        yy, xx = (y + 4 + i * h + j * g) % NY, (x + 4 + i * g + j * h) % NX
        got(table_ref.at[yy, :, xx, :, pcols], pr.at[k])

    def share(i, j):
        k = len(seen)
        seen.append((i, j))
        send(chunk(i, j), chunk(i, j), ps.at[k], pr.at[k], partner)

    def out(row, here, along, far):
        send(here, here, as_.at[row, 0], ar.at[row, 0], along(1))
        send(here, here, as_.at[row, 1], ar.at[row, 1], along(-1))
        if far:
            send(here, here, as_.at[row, 2], ar.at[row, 2], along(2))

    def first(i):
        return to(i, 0)

    def second(i):
        return to(0, i)

    out(0, chunk(0, 0), first, True)
    out(1, chunk(0, 0), second, False)
    share(0, 0)
    for c in range(4):
        gram_ref[c] = gram(g * 4 + c)
    got(chunk(-1, 0), ar.at[0, 0])
    out(2, chunk(-1, 0), second, False)
    got(chunk(1, 0), ar.at[0, 1])
    out(3, chunk(1, 0), second, False)
    share(-1, 0)
    share(1, 0)

    def pass_on(row, i):
        got(chunk(i, -1), ar.at[row, 0])
        lo = chunk(i, -1, 0, 4)
        send(lo, lo, as_.at[row, 2], ar.at[row, 2], to(0, 1))
        got(chunk(i, 1), ar.at[row, 1])
        hi = chunk(i, 1, 4, 4)
        send(hi, hi, as_.at[row, 3], ar.at[row, 3], to(0, -1))
        share(i, -1)
        share(i, 1)

    pass_on(1, 0)
    got(chunk(2, 0), ar.at[0, 2])
    out(4, chunk(2, 0), second, True)
    share(2, 0)
    pass_on(2, -1)
    pass_on(3, 1)
    got(ogram, pgr)
    for c in range(4):
        one = jnp.sum(jnp.where(iota((8, 1), 0) == g * 4 + c, denom, 0.0), axis=0, keepdims=True)
        gram_ref[c] = (gram_ref[c] + ogram[c]) / one
    gram_copy = pltpu.make_async_copy(gram_ref, gram_out, outs.at[1])
    gram_copy.start()
    for row, i in ((1, 0), (2, -1), (3, 1)):
        got(chunk(i, 2, 0, 4), ar.at[row, 2])
        got(chunk(i, 2, 4, 4), ar.at[row, 3])
        share(i, 2)
    for n, i in enumerate((-1, 1, 2)):
        got(chunk(2, i), ar.at[4, n])
        share(2, i)
    for k in range(16):
        take(k)
    hot_copy.wait()
    gram_copy.wait()
    got(sendbuf.at[pl.ds(0, CHIPS - 1)], a2s)
    for c in sent:
        c.wait_send()


def route(embeddings, dest, slot, centroids, rank):
    dma = pltpu.SemaphoreType.DMA
    vm = pltpu.VMEM
    n = embeddings.shape[0]
    return pl.pallas_call(
        routed,
        out_shape=(jax.ShapeDtypeStruct((NY, NZ, NX, 8, WIDE), BF16), jax.ShapeDtypeStruct((4, SM, SM), F32),
                   jax.ShapeDtypeStruct((1024, 1024), BF16)),
        in_specs=[pl.BlockSpec(memory_space=pltpu.HBM)] * 5,
        out_specs=(pl.BlockSpec(memory_space=pl.ANY),) * 3,
        scratch_shapes=[
            vm(embeddings.shape, BF16), vm(dest.shape, jnp.int32), vm(slot.shape, jnp.int32), vm(centroids.shape, BF16),
            vm(rank.shape, jnp.int32), vm((4, SM, SM), F32), vm((1024, 1024), BF16),
            vm((CHIPS, 8, SM), BF16), vm((CHIPS, 8, SM), BF16),
            vm((n, 256), BF16), vm((n, 256), BF16), vm((8, n), F32), vm((8, n), F32),
            vm((4, 4, NZ, 8, 512), F32),
            vm((2, 2, NZ, 8, 512), F32), vm((2, 4, NZ, 8, 512), F32),
            vm((3, NZ, 8, 512), F32),
            vm((NZ - 1, 8, 512), F32), vm((8, HALF), BF16), vm((8, HALF), F32), vm((8, HALF), F32),
            vm((4, SM, SM), F32), vm((4, SM, SM), F32),
            dma((2,)), dma, dma, dma((3,)), dma((3,)), dma((6,)), dma((6,)), dma((3,)), dma((3,)),
            dma((7,)), dma((7,)), dma, dma, dma, dma,
            dma((7,)), dma((7,)), dma((5, 4)), dma((5, 4)), dma((16,)), dma((16,)), dma((2,)), dma((5,)),
        ],
        compiler_params=pltpu.CompilerParams(collective_id=1, has_side_effects=True, vmem_limit_bytes=32 * 2**20),
        name="routed",
    )(*(pltpu.with_memory_space_constraint(v, pltpu.HBM) for v in (embeddings, dest, slot, centroids, rank)))


PARTS = (
    (0, ((512, 896), (1408, 1536))),
    (512, ((0, 256),)),
    (768, ((1536, 1792),)),
    (1024, ((256, 512),)),
    (1280, ((896, 1408),)),
)


def permuted(hot_ref, table_ref, gram_ref, out_ref, moment_ref):
    moment_ref[...] = gram_ref[...]
    hot = hot_ref[...]
    for at, spans in PARTS:
        cols = [table_ref[:, lo:hi] for lo, hi in spans]
        cols = cols[0] if len(cols) == 1 else jnp.concatenate(cols, axis=1)
        out_ref[:, at:at + cols.shape[1]] = jnp.dot(hot, cols, preferred_element_type=F32).astype(BF16)


def permute(table, hot, gram):
    k = table.shape[0]
    one = pl.BlockSpec((1, SM, SM), lambda j: (j, 0, 0))
    return pl.pallas_call(
        permuted,
        grid=(4,),
        in_specs=[
            pl.BlockSpec((k // 4, k), lambda j: (j, 0)),
            pl.BlockSpec((k, WIDE), lambda j: (0, 0)),
            one,
        ],
        out_specs=(pl.BlockSpec((k // 4, WIDE), lambda j: (j, 0)), one),
        out_shape=(jax.ShapeDtypeStruct((k, WIDE), BF16), jax.ShapeDtypeStruct(gram.shape, F32)),
        compiler_params=pltpu.CompilerParams(vmem_limit_bytes=20 * 2**20),
        name="permuted",
    )(hot, table, gram)


def on_device(embeddings, owner_dest, cluster_slot, cluster_rank, centroids):
    n = embeddings.shape[0]
    k = cluster_rank.shape[0]
    table, gram, hot = route(embeddings, owner_dest.reshape(1, n), cluster_slot.reshape(1, n), centroids,
                             cluster_rank.reshape(1, k))
    return permute(table.reshape(k, WIDE), hot, gram)


def solution(mesh):
    placed = (
        P(("dp", "grp"), None),
        P(("dp", "grp"), None),
        P(("dp", "grp"), None),
        P(),
        P("dp", None),
    )
    return jax.shard_map(
        on_device,
        mesh=mesh,
        in_specs=placed,
        out_specs=(P(), P(("dp", "grp"), None, None)),
        check_vma=False,
    )
```

```python
import functools

import jax
import jax.numpy as jnp
from jax import lax
from jax.experimental import pallas as pl
from jax.experimental.pallas import tpu as pltpu
from jax.sharding import PartitionSpec as P

WIDE = 1792
HALF = 896
NX, NY, NZ = 4, 4, 8
CHIPS = 128
SM = 256
MESH = pl.DeviceIdType.MESH
F32 = jnp.float32
BF16 = jnp.bfloat16
EPS = 1e-06


def iota(shape, dim):
    return lax.broadcasted_iota(jnp.int32, shape, dim)


def thirds(v):
    hi = v.astype(BF16)
    rest = v - hi.astype(F32)
    mid = rest.astype(BF16)
    return hi, mid, (rest - mid.astype(F32)).astype(BF16)


def row_of(col):
    n = col.shape[0]
    eye = iota((n, n), 0) == iota((n, n), 1)
    return jnp.sum(jnp.where(eye, col, 0.0), axis=0, keepdims=True)


def col_of(row):
    n = row.shape[1]
    eye = iota((n, n), 0) == iota((n, n), 1)
    return jnp.sum(jnp.where(eye, row, 0.0), axis=1, keepdims=True)


def scales(rows):
    sq = rows * rows
    s512 = jnp.sum(sq[:, :512], axis=1, keepdims=True)
    s1024 = s512 + jnp.sum(sq[:, 512:], axis=1, keepdims=True)
    return lax.rsqrt(s512 * (1.0 / 512) + EPS), lax.rsqrt(s1024 * (1.0 / 1024) + EPS)


def bits(mask):
    return mask.astype(F32).astype(BF16)


def pack(emb_ref, dest, slot, r512, r1024, sendbuf):
    n = dest.shape[1]
    hits = iota((CHIPS, n), 0) == dest
    owner = bits(hits)
    earlier = bits(iota((n, n), 0) < iota((n, n), 1))
    before = jnp.dot(owner, earlier, preferred_element_type=F32)
    pos = jnp.sum(jnp.where(hits, before, 0.0), axis=0, keepdims=True).astype(jnp.int32)
    values = [slot.astype(F32) + 1.0]
    for s in (r512, r1024):
        values += [t.astype(F32) for t in thirds(s)]
    line = iota((128, n), 0)
    tags = jnp.zeros((128, n), F32)
    for i, v in enumerate(values):
        tags = jnp.where((line & 15) == i, v, tags)
    tags = jnp.where((line >> 4) == pos, tags, 0.0).astype(BF16)
    tags = lax.dot_general(owner, tags, (((1,), (1,)), ((), ())), preferred_element_type=F32)
    place = bits(iota((CHIPS * 8, n), 0) == dest * 8 + pos)
    rows = jnp.dot(place, emb_ref[:, :SM], preferred_element_type=F32).reshape(CHIPS, 8, SM)
    wide = jnp.concatenate([tags, jnp.zeros((CHIPS, SM - 128), F32)], axis=1)
    rows = jnp.where(iota((CHIPS, 8, SM), 1) == 6, wide[:, None, :], rows)
    sendbuf[...] = rows.astype(BF16)


def order_of(dest, slot, g):
    xx, zz, yy = dest & 3, (dest >> 2) & 7, dest >> 5
    a = xx * (1 - g) + yy * g
    b = yy * (1 - g) + xx * g
    return ((a * 4 + b) * 8 + zz) * 8 + slot


def columns(g):
    return (pl.ds(pl.multiple_of(256 + g * 256, 256), 256), pl.ds(pl.multiple_of(256 + g * 512, 256), 256))


def whole(order, xs, ss, total, add):
    k = 8 * CHIPS
    hot = bits(iota((k, order.shape[1]), 0) == order)
    hot = jnp.concatenate([hot, hot, hot], axis=1)
    for at, x, s in zip((0, 256), xs, ss):
        acc = jnp.dot(hot, jnp.concatenate(thirds(x.astype(F32) * s), axis=0), preferred_element_type=F32)
        acc = acc.reshape(4, 4, NZ, 8, 256)
        if add:
            acc = acc + total[:, :, :, :, at:at + 256]
        total[:, :, :, :, at:at + 256] = acc


def routed(emb_in, dest_in, slot_in, cent_in, rank_in, table_ref, gram_out, hot_out,
           emb_ref, dest_ref, slot_ref, cent_ref, rank_ref, gram_ref, hot_ref,
           sendbuf, recvbuf, pxa, pxb, info, pinfo, total, half1, full1, full2, zgot, blk, psums, osums,
           pgram, ogram,
           own_sem, a2s, a2r, xs, xr, r1s, r1r, r2s, r2r, z3s, z3r, pss, psr, pgs, pgr,
           zs, zr, as_, ar, ps, pr, outs, ins):
    dp = lax.axis_index("dp")
    g = lax.axis_index("grp")
    x = dp % NX
    z = (dp // NX) % NZ
    y = dp // (NX * NZ)
    h = 1 - g
    partner = (dp, h)
    loads = [pltpu.make_async_copy(src, dst, ins.at[i]) for i, (src, dst) in enumerate(
        ((emb_in, emb_ref), (dest_in, dest_ref), (slot_in, slot_ref), (cent_in, cent_ref), (rank_in, rank_ref)))]
    for c in loads:
        c.start()
    barrier = pltpu.get_barrier_semaphore()
    pl.semaphore_signal(barrier, inc=1, device_id=partner, device_id_type=MESH)

    xs4 = [(x + 2 + k) % NX for k in range(4)]

    def others(body):
        def along(first, last, base, ks):
            def step(j, c):
                at = (base + (z + 4 + j) % NZ) * NX
                for k in ks:
                    body(at + xs4[k])
                return c
            lax.fori_loop(first, last, step, 0)

        for i in range(NY):
            base = ((y + 2 + i) % NY) * NZ
            if i == 2:
                along(0, NZ, base, (0, 1, 3))
                along(0, 4, base, (2,))
                along(5, NZ, base, (2,))
            else:
                along(0, NZ, base, range(4))

    def greet(t):
        pl.semaphore_signal(barrier, inc=1, device_id=(t, g), device_id_type=MESH)

    others(greet)
    for c in loads:
        c.wait()
    dest, slot = dest_ref[...], slot_ref[...]
    c512, c1024 = scales(emb_ref[...].astype(F32))
    r512, r1024 = row_of(c512), row_of(c1024)
    gf = g.astype(F32)
    info[...] = jnp.zeros_like(info)
    info[0:1, :] = order_of(dest, slot, h).astype(F32)
    info[1:2, :] = r512 * gf + r1024 * (1.0 - gf)
    info[2:3, :] = r1024
    ca, cb = columns(g)
    whole(order_of(dest, slot, g), (emb_ref[:, ca], emb_ref[:, cb]), (c512 * (1.0 - gf) + c1024 * gf, c1024), total, False)
    pl.semaphore_wait(barrier, CHIPS)

    sent = []

    def send(src, dst, ss, rs, peer):
        c = pltpu.make_async_remote_copy(src_ref=src, dst_ref=dst, send_sem=ss, recv_sem=rs,
                                         device_id=peer, device_id_type=MESH)
        c.start()
        sent.append(c)

    def got(ref, sem):
        pltpu.make_async_copy(ref, ref, sem).wait()

    pa, pb = columns(h)
    send(info, pinfo, xs.at[0], xr.at[0], partner)
    send(emb_ref.at[:, pa], pxa, xs.at[1], xr.at[1], partner)
    send(emb_ref.at[:, pb], pxb, xs.at[2], xr.at[2], partner)
    pack(emb_ref, dest, slot, r512, r1024, sendbuf)
    mine = pltpu.make_async_copy(sendbuf.at[dp], recvbuf.at[dp], own_sem.at[0])
    mine.start()
    got(pinfo, xr.at[0])
    got(pxa, xr.at[1])
    got(pxb, xr.at[2])
    whole(pinfo[0:1, :].astype(jnp.int32), (pxa[...], pxb[...]), (col_of(pinfo[1:2, :]), col_of(pinfo[2:3, :])), total, True)

    def scatter(t):
        pltpu.make_async_remote_copy(src_ref=sendbuf.at[t], dst_ref=recvbuf.at[dp], send_sem=a2s, recv_sem=a2r,
                                     device_id=(t, g), device_id_type=MESH).start()

    def to(i, j):
        yy, xx = (y + 4 + i * g + j * h) % NY, (x + 4 + i * h + j * g) % NX
        return ((yy * NZ + z) * NX + xx, g)

    p = x * h + y * g
    q = y * h + x * g

    def ring(at, me, lo, hi, half, full, plus, minus, ss, rs, between):
        up, down, far = (me + 1) % 4, (me + 3) % 4, (me + 2) % 4
        send(at(far, lo), half.at[0], ss.at[0], rs.at[0], plus)
        send(at(far, hi), half.at[1], ss.at[1], rs.at[1], minus)
        send(at(up, hi), full.at[0, hi], ss.at[2], rs.at[2], plus)
        send(at(down, lo), full.at[1, lo], ss.at[3], rs.at[3], minus)
        got(half.at[0], rs.at[0])
        ref = at(up, lo)
        ref[...] = ref[...] + half[0]
        send(ref, full.at[0, lo], ss.at[4], rs.at[4], plus)
        got(half.at[1], rs.at[1])
        ref = at(down, hi)
        ref[...] = ref[...] + half[1]
        send(ref, full.at[1, hi], ss.at[5], rs.at[5], minus)
        between()
        got(full.at[0, hi], rs.at[2])
        got(full.at[1, lo], rs.at[3])
        got(full.at[0, lo], rs.at[4])
        got(full.at[1, hi], rs.at[5])
        for part in (lo, hi):
            ref = at(me, part)
            ref[...] = ref[...] + full[0, part] + full[1, part]

    ring(lambda i, s: total.at[i, s], p, pl.ds(0, 2), pl.ds(2, 2), half1, full1, to(1, 0), to(-1, 0), r1s, r1r,
         lambda: others(scatter))
    for i in (2, 1, 3):
        send(total.at[p, (q + i) % 4], full2.at[i - 1], r2s.at[i - 1], r2r.at[i - 1], to(0, i))
    for i in (1, 3, 2):
        got(full2.at[i - 1], r2r.at[i - 1])
    total[p, q] = total[p, q] + full2[0] + full2[1] + full2[2]

    def along_z(d):
        return ((y * NZ + (z + d) % NZ) * NX + x, g)

    for d in range(1, NZ):
        send(total.at[p, q, (z + d) % NZ], zgot.at[d - 1], z3s.at[d - 1], z3r.at[d - 1], along_z(d))

    mine.wait()
    every = recvbuf.at[pl.ds(0, CHIPS - 1)]
    got(every, a2r)
    rows = recvbuf[...].astype(F32)
    slots = CHIPS * 8
    tags = jnp.broadcast_to(rows[:, 6:7, :128], (CHIPS, 8, 128)).reshape(slots, 128)
    lane = iota((slots, 128), 1)
    tags = jnp.where((lane >> 4) == (iota((slots, 128), 0) & 7), tags, 0.0).astype(BF16)
    f = iota((128, 128), 0) & 15
    c = iota((128, 128), 1)
    pick = ((f == 0) & (c == 0)) | ((f >= 1) & (f <= 3) & (c == 1)) | ((f >= 4) & (f <= 6) & (c == 2))
    vals = jnp.dot(tags, pick.astype(F32).astype(BF16), preferred_element_type=F32)
    idrow = vals.T[0:1, :]
    selt = (idrow == (iota((8, slots), 0) + 1).astype(F32)).astype(F32)
    sel = (vals[:, 0:1] == (iota((slots, 8), 1) + 1).astype(F32)).astype(F32).astype(BF16)
    cent = jnp.dot(sel, cent_ref[:, :SM], preferred_element_type=F32)
    rows = rows.reshape(slots, SM)
    s256 = lax.rsqrt(jnp.sum(rows * rows, axis=1, keepdims=True) * (1.0 / 256) + EPS)
    small = (rows * s256 - cent).astype(BF16)
    seltb = selt.astype(BF16)
    osums[:, 0:256] = jnp.dot(seltb, small, preferred_element_type=F32)
    osums[:, 256:512] = jnp.dot(seltb, (rows * vals[:, 1:2] - cent).astype(BF16), preferred_element_type=F32)
    osums[:, 512:768] = jnp.dot(seltb, (rows * vals[:, 2:3] - cent).astype(BF16), preferred_element_type=F32)
    osums[:, 768:896] = jnp.broadcast_to(jnp.sum(selt, axis=1, keepdims=True), (8, 128))
    send(osums, psums, pss, psr, partner)
    smallt = small.astype(F32).T

    def gram(c):
        keep = idrow == (c + 1).astype(F32)
        return jnp.dot(jnp.where(keep, smallt, 0.0).astype(BF16), small, preferred_element_type=F32)

    for d in range(1, NZ):
        got(zgot.at[d - 1], z3r.at[d - 1])
    got(psums, psr)
    sums = osums[...] + psums[...]
    count = sums[:, 768:769]
    denom = count + 1.0
    big = total[p, q, z]
    for d in range(1, NZ):
        big = big + zgot[d - 1]
    blk[:, 0:256] = ((big[:, :256] - count * cent_ref[:, ca].astype(F32)) / denom).astype(BF16)
    blk[:, 256:512] = ((big[:, 256:] - count * cent_ref[:, cb].astype(F32)) / denom).astype(BF16)
    part = jnp.where(gf > 0.5, sums[:, 384:768], sums[:, 0:384])
    blk[:, 512:896] = (part / denom).astype(BF16)

    cols = pl.ds(pl.multiple_of(g * HALF, 128), HALF)
    pcols = pl.ds(pl.multiple_of(h * HALF, 128), HALF)

    def chunk(i, j, z0=0, nz=NZ, at=cols):
        yy, xx = (y + 4 + i * g + j * h) % NY, (x + 4 + i * h + j * g) % NX
        return table_ref.at[yy, pl.ds(z0, nz), xx, :, at]

    home = table_ref.at[y, z, x, :, cols]
    for d in range(1, NZ):
        send(blk, home, zs.at[d - 1], zr.at[d - 1], along_z(d))
    own = pltpu.make_async_copy(blk, home, own_sem.at[1])
    own.start()
    for c in range(4):
        pgram[c] = gram(h * 4 + c)
    send(pgram, ogram, pgs, pgr, partner)
    for b in range(8):
        piece = rank_ref[:, b * 128:(b + 1) * 128].astype(F32)
        col = col_of(piece).astype(jnp.int32)
        hot_ref[b * 128:(b + 1) * 128, :] = bits(iota((128, 1024), 1) == col)
    hot_copy = pltpu.make_async_copy(hot_ref, hot_out, outs.at[0])
    hot_copy.start()
    own.wait()
    for d in range(1, NZ):
        got(home, zr.at[d - 1])

    seen = []

    def take(k):
        i, j = seen[k]
        yy, xx = (y + 4 + i * h + j * g) % NY, (x + 4 + i * g + j * h) % NX
        got(table_ref.at[yy, :, xx, :, pcols], pr.at[k])

    def share(i, j):
        k = len(seen)
        seen.append((i, j))
        send(chunk(i, j), chunk(i, j), ps.at[k], pr.at[k], partner)

    def out(row, here, along, far):
        send(here, here, as_.at[row, 0], ar.at[row, 0], along(1))
        send(here, here, as_.at[row, 1], ar.at[row, 1], along(-1))
        if far:
            send(here, here, as_.at[row, 2], ar.at[row, 2], along(2))

    def first(i):
        return to(i, 0)

    def second(i):
        return to(0, i)

    out(0, chunk(0, 0), first, True)
    out(1, chunk(0, 0), second, False)
    share(0, 0)
    for c in range(4):
        gram_ref[c] = gram(g * 4 + c)
    got(chunk(-1, 0), ar.at[0, 0])
    out(2, chunk(-1, 0), second, False)
    got(chunk(1, 0), ar.at[0, 1])
    out(3, chunk(1, 0), second, False)
    share(-1, 0)
    share(1, 0)

    def pass_on(row, i):
        got(chunk(i, -1), ar.at[row, 0])
        lo = chunk(i, -1, 0, 4)
        send(lo, lo, as_.at[row, 2], ar.at[row, 2], to(0, 1))
        got(chunk(i, 1), ar.at[row, 1])
        hi = chunk(i, 1, 4, 4)
        send(hi, hi, as_.at[row, 3], ar.at[row, 3], to(0, -1))
        share(i, -1)
        share(i, 1)

    pass_on(1, 0)
    got(chunk(2, 0), ar.at[0, 2])
    out(4, chunk(2, 0), second, True)
    share(2, 0)
    got(ogram, pgr)
    for c in range(4):
        one = jnp.sum(jnp.where(iota((8, 1), 0) == g * 4 + c, denom, 0.0), axis=0, keepdims=True)
        gram_ref[c] = (gram_ref[c] + ogram[c]) / one
    gram_copy = pltpu.make_async_copy(gram_ref, gram_out, outs.at[1])
    gram_copy.start()
    pass_on(2, -1)
    pass_on(3, 1)
    for row, i in ((1, 0), (2, -1), (3, 1)):
        got(chunk(i, 2, 0, 4), ar.at[row, 2])
        got(chunk(i, 2, 4, 4), ar.at[row, 3])
        share(i, 2)
    for n, i in enumerate((-1, 1, 2)):
        got(chunk(2, i), ar.at[4, n])
        share(2, i)
    for k in range(16):
        take(k)
    hot_copy.wait()
    gram_copy.wait()
    got(sendbuf.at[pl.ds(0, CHIPS - 1)], a2s)
    for c in sent:
        c.wait_send()


def route(embeddings, dest, slot, centroids, rank):
    dma = pltpu.SemaphoreType.DMA
    vm = pltpu.VMEM
    n = embeddings.shape[0]
    return pl.pallas_call(
        routed,
        out_shape=(jax.ShapeDtypeStruct((NY, NZ, NX, 8, WIDE), BF16), jax.ShapeDtypeStruct((4, SM, SM), F32),
                   jax.ShapeDtypeStruct((1024, 1024), BF16)),
        in_specs=[pl.BlockSpec(memory_space=pltpu.HBM)] * 5,
        out_specs=(pl.BlockSpec(memory_space=pl.ANY),) * 3,
        scratch_shapes=[
            vm(embeddings.shape, BF16), vm(dest.shape, jnp.int32), vm(slot.shape, jnp.int32), vm(centroids.shape, BF16),
            vm(rank.shape, jnp.int32), vm((4, SM, SM), F32), vm((1024, 1024), BF16),
            vm((CHIPS, 8, SM), BF16), vm((CHIPS, 8, SM), BF16),
            vm((n, 256), BF16), vm((n, 256), BF16), vm((8, n), F32), vm((8, n), F32),
            vm((4, 4, NZ, 8, 512), F32),
            vm((2, 2, NZ, 8, 512), F32), vm((2, 4, NZ, 8, 512), F32),
            vm((3, NZ, 8, 512), F32),
            vm((NZ - 1, 8, 512), F32), vm((8, HALF), BF16), vm((8, HALF), F32), vm((8, HALF), F32),
            vm((4, SM, SM), F32), vm((4, SM, SM), F32),
            dma((2,)), dma, dma, dma((3,)), dma((3,)), dma((6,)), dma((6,)), dma((3,)), dma((3,)),
            dma((7,)), dma((7,)), dma, dma, dma, dma,
            dma((7,)), dma((7,)), dma((5, 4)), dma((5, 4)), dma((16,)), dma((16,)), dma((2,)), dma((5,)),
        ],
        compiler_params=pltpu.CompilerParams(collective_id=1, has_side_effects=True, vmem_limit_bytes=32 * 2**20),
        name="routed",
    )(*(pltpu.with_memory_space_constraint(v, pltpu.HBM) for v in (embeddings, dest, slot, centroids, rank)))


PARTS = (
    (0, ((512, 896), (1408, 1536))),
    (512, ((0, 256),)),
    (768, ((1536, 1792),)),
    (1024, ((256, 512),)),
    (1280, ((896, 1408),)),
)


def permuted(hot_ref, table_ref, gram_ref, out_ref, moment_ref, buf, sems):
    moments = pltpu.make_async_copy(gram_ref, moment_ref, sems.at[4])
    moments.start()
    copies = []
    for j in range(4):
        rows = pl.ds(j * 256, 256)
        hot = hot_ref[rows, :]
        for at, spans in PARTS:
            cols = [table_ref[:, lo:hi] for lo, hi in spans]
            cols = cols[0] if len(cols) == 1 else jnp.concatenate(cols, axis=1)
            buf[rows, at:at + cols.shape[1]] = jnp.dot(hot, cols, preferred_element_type=F32).astype(BF16)
        copies.append(pltpu.make_async_copy(buf.at[rows], out_ref.at[rows], sems.at[j]))
        copies[-1].start()
    for c in copies:
        c.wait()
    moments.wait()


def permute(table, hot, gram):
    k = table.shape[0]
    return pl.pallas_call(
        permuted,
        in_specs=[pl.BlockSpec(memory_space=pltpu.VMEM)] * 3,
        out_specs=(pl.BlockSpec(memory_space=pltpu.HBM),) * 2,
        out_shape=(jax.ShapeDtypeStruct((k, WIDE), BF16), jax.ShapeDtypeStruct(gram.shape, F32)),
        scratch_shapes=[pltpu.VMEM((k, WIDE), BF16), pltpu.SemaphoreType.DMA((5,))],
        compiler_params=pltpu.CompilerParams(vmem_limit_bytes=20 * 2**20),
        name="permuted",
    )(hot, table, gram)


def on_device(embeddings, owner_dest, cluster_slot, cluster_rank, centroids):
    n = embeddings.shape[0]
    k = cluster_rank.shape[0]
    table, gram, hot = route(embeddings, owner_dest.reshape(1, n), cluster_slot.reshape(1, n), centroids,
                             cluster_rank.reshape(1, k))
    return permute(table.reshape(k, WIDE), hot, gram)


def solution(mesh):
    placed = (
        P(("dp", "grp"), None),
        P(("dp", "grp"), None),
        P(("dp", "grp"), None),
        P(),
        P("dp", None),
    )
    return jax.shard_map(
        on_device,
        mesh=mesh,
        in_specs=placed,
        out_specs=(P(), P(("dp", "grp"), None, None)),
        check_vma=False,
    )
```
